32 devices in a mesh: dp: 4 (over y, x), wide: 8 (over z, core).
Axes of the slice: x: 2, y: 2, z: 4, core: 2. Of those that a mesh axis runs over, the one named last changes fastest.
Arguments:
- source_ids: int32 [32, 256], replicated, may hold values from 0 to 32767
- token_ids: int32 [32, 256], replicated, may hold values from 0 to 32767
- targets: int32 [32, 256], replicated, may hold values from 0 to 32767
- pad_mask: int32 [32, 256], replicated, may hold values from 0 to 1, as said below
- pass_widths: int32 [2], replicated, may hold values from 768 to 3072, as said below
- attn_master: float32 [3, 640, 2048], P(None, ('dp', 'wide'))
- attn_m: float32 [3, 640, 2048], P(None, ('dp', 'wide')), may hold values from -5.9604645e-07 to 5.9604645e-07
- attn_v: float32 [3, 640, 2048], P(None, ('dp', 'wide'))
- norm_params: float32 [14, 640], replicated
- norm_m: float32 [14, 640], replicated, may hold values from -2.861023e-06 to 2.861023e-06
- norm_v: float32 [14, 640], replicated
- up_master: float32 [2, 640, 3072], P(None, None, 'wide'), may hold values from -0.25 to 0.25
- up_m: float32 [2, 640, 3072], P(None, None, 'wide'), may hold values from -5.9604645e-07 to 5.9604645e-07
- up_v: float32 [2, 640, 3072], P(None, None, 'wide')
- down_master: float32 [2, 3072, 640], P(None, 'wide'), may hold values from -0.21875 to 0.21875
- down_m: float32 [2, 3072, 640], P(None, 'wide'), may hold values from -5.9604645e-07 to 5.9604645e-07
- down_v: float32 [2, 3072, 640], P(None, 'wide')
- embed_master: float32 [32768, 640], P('wide'), may hold values from -0.25 to 0.25
- embed_m: float32 [32768, 640], P('wide'), may hold values from -5.9604645e-07 to 5.9604645e-07
- embed_v: float32 [32768, 640], P('wide')
- ema_old: float32 [32768, 640], P('wide', 'dp'), may hold values from -0.25 to 0.25
Outputs:
- losses: float32 [2], replicated
- row_losses: float32 [2, 32, 256], P(None, ('dp', 'wide'))
- grad_norm: float32 [1], replicated
- attn_new: float32 [3, 640, 2048], P(None, ('dp', 'wide'))
- attn_m_new: float32 [3, 640, 2048], P(None, ('dp', 'wide'))
- attn_v_new: float32 [3, 640, 2048], P(None, ('dp', 'wide'))
- norm_new: float32 [14, 640], replicated
- norm_m_new: float32 [14, 640], replicated
- norm_v_new: float32 [14, 640], replicated
- up_new: float32 [2, 640, 3072], P(None, None, 'wide')
- up_m_new: float32 [2, 640, 3072], P(None, None, 'wide')
- up_v_new: float32 [2, 640, 3072], P(None, None, 'wide')
- down_new: float32 [2, 3072, 640], P(None, 'wide')
- down_m_new: float32 [2, 3072, 640], P(None, 'wide')
- down_v_new: float32 [2, 3072, 640], P(None, 'wide')
- embed_new: float32 [32768, 640], P('wide')
- embed_m_new: float32 [32768, 640], P('wide')
- embed_v_new: float32 [32768, 640], P('wide')
- ema_new: float32 [32768, 640], P('wide', 'dp')
- attn_half: bfloat16 [3, 640, 2048], P(None, ('dp', 'wide'))
- up_half: bfloat16 [2, 640, 3072], P(None, None, 'wide')
- down_half: bfloat16 [2, 3072, 640], P(None, 'wide')
- embed_half: bfloat16 [32768, 640], P('wide')
The draws below stay inside these ranges and needn't reach their ends.
Inputs may be any that keep to these rules, and one draw needn't show every extreme that they name: `pad_mask`: each pair's mask is 1 on a prefix of 64 or more positions and 0 after it; it serves the source and the target alike. `pass_widths`: entry 0 is 3072; entry 1 is a multiple of 8 from 768 to 1536.
All inputs are finite; a program needn't handle non-finite values.
Results may differ from the reference program's by a relative error of at most 0.0067.
Values may be sent and summed in bfloat16 or wider, within the bound.
A program may use at most 320 MiB of HBM per device.

```python
import math
import jax
import jax.numpy as jnp
import numpy as np
from jax import lax

D = 640
HEADS = 8
HEAD = 64
QKV = 512
FF = 3072
V = 32768
L = 256
SEQS = 32


def second_moment(key, shape, factor):
    spread = jnp.exp(jax.random.uniform(key, shape, jnp.float32, math.log(0.5), math.log(8.0)))
    params_all = 12 * D * QKV + 4 * D * FF + V * D
    return spread * (factor * 0.0204 * 2.5e-05 / params_all)


def draw_pad_mask(key, part):
    lengths = jax.random.randint(key, (SEQS, 1), L // 4, L + 1)
    return (jnp.arange(L)[None, :] < lengths).astype(jnp.int32)


def draw_pass_widths(key, part):
    smaller = 8 * jax.random.randint(key, (), FF // 32, FF // 16 + 1)
    return jnp.stack([jnp.int32(FF), smaller.astype(jnp.int32)])


def draw_attn_master(key, part):
    base = jax.random.normal(key, (3, D, 4 * QKV), jnp.float32)
    column = jnp.arange(4 * QKV)[None, None, :]
    return jnp.where(column < 3 * QKV, base * D ** (-0.5), base * (4.0 * QKV ** (-0.5)))


def draw_norm_params(key, part):
    noise = jax.random.normal(key, (14, D), jnp.float32)
    row_index = jnp.arange(14)[:, None]
    return jnp.where(row_index < 7, 1.0 + 0.1 * jnp.clip(noise, -4.0, 4.0), 0.2 * noise)


def draw_attn_v(key, part):
    return second_moment(key, (3, D, 4 * QKV), 1.0)


def draw_norm_v(key, part):
    return second_moment(key, (14, D), 25.0)


def draw_up_v(key, part):
    return second_moment(key, (2, D, FF), 1.0)


def draw_down_v(key, part):
    return second_moment(key, (2, FF, D), 1.0)


def draw_embed_v(key, part):
    return second_moment(key, (V, D), 1.0)


def with_ends(drawn, rng, low, high):
    extent = drawn.shape
    index_at = [jax.random.randint(jax.random.fold_in(rng, axis), (), 0, extent[axis]) for axis in range(len(extent))]
    drawn = drawn.at[tuple(index_at)].set(low)
    longest = extent.index(max(extent))
    index_at[longest] = (index_at[longest] + 1) % extent[longest]
    return drawn.at[tuple(index_at)].set(high)


def block_scale(stream_key, dims, shards, smallest, top_value):
    level, own = 1.0, jax.random.fold_in(stream_key, 6)
    for dim, blocks in shards:
        draws = jnp.exp(jax.random.uniform(jax.random.fold_in(own, dim), (blocks,), jnp.float32, smallest / len(shards), top_value / len(shards)))
        level = level * jnp.repeat(draws, dims[dim] // blocks).reshape([-1 if axis == dim else 1 for axis in range(len(dims))])
    return level


def rank_bounds(count, skew):
    portions = [(1 << 20) // math.isqrt(standing ** skew) + 1 for standing in range(1, count + 1)]
    deviation = 1 + sum(portions) // (1 << 30)
    return np.cumsum(np.array([max(1, weight // deviation) for weight in portions]))


def ranked_ids(own_key, extent, count, skew):
    table = rank_bounds(count, skew)
    pick = jax.random.randint(jax.random.fold_in(own_key, 1), extent, 0, int(table[count - 1]))
    standing = jnp.searchsorted(jnp.asarray(table, jnp.int32), pick, side="right")
    return jax.random.permutation(jax.random.fold_in(own_key, 2), count)[standing].astype(jnp.int32)


def centred(key, dims, width, bound, pieces=(), held_as=jnp.bfloat16):
    drawn = width * jax.random.normal(key, dims, jnp.float32)
    if pieces:
        drawn = drawn * block_scale(key, dims, pieces, -0.22, 0.18)
    return jnp.clip(drawn, -bound, bound).astype(held_as)


def setup_inputs(seed: int = 0) -> dict:
    splits = jax.random.split(jax.random.key(seed), 22)
    source_ids = with_ends(ranked_ids(splits[0], (SEQS, L), V, 2), jax.random.fold_in(splits[0], 3), 0, V - 1).astype(jnp.int32)
    token_ids = with_ends(ranked_ids(splits[1], (SEQS, L), V, 2), jax.random.fold_in(splits[1], 3), 0, V - 1).astype(jnp.int32)
    targets = with_ends(ranked_ids(splits[2], (SEQS, L), V, 2), jax.random.fold_in(splits[2], 3), 0, V - 1).astype(jnp.int32)
    pad_mask = draw_pad_mask(jax.random.fold_in(splits[21], 71), 0)
    pass_widths = draw_pass_widths(jax.random.fold_in(splits[21], 71), 0)
    attn_master = draw_attn_master(jax.random.fold_in(splits[21], 71), 0)
    attn_m = centred(splits[6], (3, D, 4 * QKV), ((12 * D * QKV + 4 * D * FF + V * D) * 3305785) ** -0.5, 5.960464477539062e-07, ((1, 32),), jnp.float32)
    attn_v = draw_attn_v(jax.random.fold_in(splits[21], 71), 0)
    norm_params = draw_norm_params(jax.random.fold_in(splits[21], 71), 0)
    norm_m = centred(splits[9], (14, D), ((12 * D * QKV + 4 * D * FF + V * D) * 132231) ** -0.5, 2.86102294921875e-06, (), jnp.float32)
    norm_v = draw_norm_v(jax.random.fold_in(splits[21], 71), 0)
    up_master = centred(splits[11], (2, D, FF), D ** -0.5, 0.25, ((2, 8),), jnp.float32)
    up_m = centred(splits[12], (2, D, FF), ((12 * D * QKV + 4 * D * FF + V * D) * 3305785) ** -0.5, 5.960464477539062e-07, ((2, 8),), jnp.float32)
    up_v = draw_up_v(jax.random.fold_in(splits[21], 71), 0)
    down_master = centred(splits[14], (2, FF, D), (FF // 4) ** -0.5, 0.21875, ((1, 8),), jnp.float32)
    down_m = centred(splits[15], (2, FF, D), ((12 * D * QKV + 4 * D * FF + V * D) * 3305785) ** -0.5, 5.960464477539062e-07, ((1, 8),), jnp.float32)
    down_v = draw_down_v(jax.random.fold_in(splits[21], 71), 0)
    embed_master = centred(splits[17], (V, D), D ** -0.5, 0.25, ((0, 8),), jnp.float32)
    embed_m = centred(splits[18], (V, D), ((12 * D * QKV + 4 * D * FF + V * D) * 3305785) ** -0.5, 5.960464477539062e-07, ((0, 8),), jnp.float32)
    embed_v = draw_embed_v(jax.random.fold_in(splits[21], 71), 0)
    ema_old = centred(splits[20], (V, D), D ** -0.5, 0.25, ((0, 8), (1, 4)), jnp.float32)
    return {"source_ids": source_ids, "token_ids": token_ids, "targets": targets, "pad_mask": pad_mask, "pass_widths": pass_widths, "attn_master": attn_master, "attn_m": attn_m, "attn_v": attn_v, "norm_params": norm_params, "norm_m": norm_m, "norm_v": norm_v, "up_master": up_master, "up_m": up_m, "up_v": up_v, "down_master": down_master, "down_m": down_m, "down_v": down_v, "embed_master": embed_master, "embed_m": embed_m, "embed_v": embed_v, "ema_old": ema_old}


@jax.custom_vjp
def low(v):
    return lax.optimization_barrier(v.astype(jnp.bfloat16)).astype(jnp.float32)

@jax.custom_vjp
def low_back(v):
    return v

def low_keep(v):
    return (low(v), None)

def low_pass(kept, grad):
    return (grad,)

def back_keep(v):
    return (v, None)

def back_low(kept, grad):
    return (low(grad),)
low.defvjp(low_keep, low_pass)
low_back.defvjp(back_keep, back_low)
highest = lax.Precision.HIGHEST
smooth = 0.1
norm_eps = 1e-05
clip_limit = 0.005
beta_first = 0.9
beta_second = 0.98
adam_eps = 1e-08
rate_matrix = 0.02
rate_gains = 0.2
decay_weight = 0.01
ema_decay = 0.8
norm_count = 7

def matmul(left, right):
    return jnp.dot(left, right, precision=highest, preferred_element_type=jnp.float32)

def sinusoid(length, model_width):
    places = jnp.arange(length, dtype=jnp.float32)[:, None]
    halves = jnp.arange(model_width // 2, dtype=jnp.float32)[None, :]
    angles = places * jnp.exp(halves * (-2.0 * math.log(10000.0) / model_width))
    return jnp.concatenate([jnp.sin(angles), jnp.cos(angles)], axis=1)

def layer_norm(values, gain, shift):
    centered = values - lax.optimization_barrier(jnp.mean(values, axis=-1, keepdims=True))
    inverse = lax.rsqrt(lax.optimization_barrier(jnp.mean(centered * centered, axis=-1, keepdims=True)) + norm_eps)
    return centered * inverse * gain + shift

def attend(q_in, kv_in, block, allowed, group_seqs):
    row_count = q_in.shape[0]
    queries = low(low_back(matmul(q_in, block[:, :QKV]))).reshape(group_seqs, L, HEADS, HEAD)
    pair = low(low_back(matmul(kv_in, block[:, QKV:3 * QKV])))
    key_rows = pair[:, :QKV].reshape(group_seqs, L, HEADS, HEAD)
    value_rows = pair[:, QKV:].reshape(group_seqs, L, HEADS, HEAD)
    scores = low_back(jnp.einsum('gqhe,gkhe->ghqk', queries, key_rows, precision=highest) * HEAD ** (-0.5))
    scores = jnp.where(allowed, scores, -1e+30)
    row_peak = lax.optimization_barrier(jnp.max(scores, axis=-1, keepdims=True))
    row_exp = jnp.exp(scores - row_peak)
    probs = low(row_exp / lax.optimization_barrier(jnp.sum(row_exp, axis=-1, keepdims=True)))
    mixed = jnp.einsum('ghqk,gkhe->gqhe', probs, value_rows, precision=highest).reshape(row_count, QKV)
    mixed = low(low_back(mixed))
    return low_back(matmul(mixed, block[:, 3 * QKV:].T))

def group_losses(params, src_block, ids_block, target_block, weight_block, mask_block, pass_widths):
    attn_w, norm_rows, up_w, down_w, emb_table = params
    group_seqs = ids_block.shape[0]
    free_mask = (mask_block > 0)[:, None, None, :]
    causal = jnp.arange(L)[:, None] >= jnp.arange(L)[None, :]
    causal_mask = free_mask & causal[None, None]
    position = jnp.tile(sinusoid(L, D), (group_seqs, 1))

    def embed(id_rows):
        return math.sqrt(D) * low_back(emb_table[id_rows.reshape(-1)]) + position

    def norm_at(values, index):
        return layer_norm(values, norm_rows[index], norm_rows[norm_count + index])
    src_in = embed(src_block)
    tgt_in = embed(ids_block)
    src_low = low(norm_at(src_in, 0))
    src_hidden = src_in + attend(src_low, src_low, attn_w[0], free_mask, group_seqs)
    src_act = low_back(matmul(low(norm_at(src_hidden, 1)), up_w[0]))
    tgt_low = low(norm_at(tgt_in, 3))
    tgt_hidden = tgt_in + attend(tgt_low, tgt_low, attn_w[1], causal_mask, group_seqs)
    cross_low = low(norm_at(tgt_hidden, 4))
    unit_ids = jnp.arange(FF)[None, :]
    mask_rows = mask_block.reshape(-1).astype(jnp.float32)
    losses = []
    per_rows = []
    for pass_index in range(2):

        def nested(inner, layer):
            active = low(jnp.where((unit_ids < pass_widths[pass_index]) & (inner > 0), inner, 0.0))
            return low_back(matmul(active, down_w[layer]))
        memory = low(norm_at(src_hidden + nested(src_act, 0), 2))
        crossed = tgt_hidden + attend(cross_low, memory, attn_w[2], free_mask, group_seqs)
        dec_act = low_back(matmul(low(norm_at(crossed, 5)), up_w[1]))
        final_low = low(norm_at(crossed + nested(dec_act, 1), 6))
        logits = low_back(matmul(final_low, emb_table.T))
        logit_peak = lax.optimization_barrier(jnp.max(logits, axis=-1, keepdims=True))
        log_total = logit_peak[:, 0] + jnp.log(lax.optimization_barrier(jnp.sum(jnp.exp(logits - logit_peak), axis=-1)))
        picked = jnp.take_along_axis(logits, target_block.reshape(-1, 1), axis=1)[:, 0]
        per_row = log_total - (1.0 - smooth) * picked - smooth / V * lax.optimization_barrier(jnp.sum(logits, axis=-1))
        losses.append(jnp.sum(weight_block.reshape(-1) * per_row))
        per_rows.append(mask_rows * per_row)
    return (jnp.stack(losses), jnp.stack(per_rows))

def adamw(weight, first_m, second_m, grad_item, step_rate):
    first_new = beta_first * first_m + (1.0 - beta_first) * grad_item
    second_new = beta_second * second_m + (1.0 - beta_second) * grad_item * grad_item
    weight_new = weight - step_rate * (first_new / (jnp.sqrt(second_new) + adam_eps) + decay_weight * weight)
    return (weight_new, first_new, second_new)

def reference(source_ids, token_ids, targets, pad_mask, pass_widths, attn_master, attn_m, attn_v, norm_params, norm_m, norm_v, up_master, up_m, up_v, down_master, down_m, down_v, embed_master, embed_m, embed_v, ema_old):

    def rounded(weight):
        return weight.astype(jnp.bfloat16).astype(jnp.float32)
    params = (rounded(attn_master), norm_params, rounded(up_master), rounded(down_master), rounded(embed_master))
    group_seqs = math.gcd(SEQS, max(1, 4096 // L))
    weights = pad_mask.astype(jnp.float32) / jnp.sum(pad_mask).astype(jnp.float32)
    blocks = (source_ids.reshape(-1, group_seqs, L), token_ids.reshape(-1, group_seqs, L), targets.reshape(-1, group_seqs, L), weights.reshape(-1, group_seqs, L), pad_mask.reshape(-1, group_seqs, L))
    checked = jax.checkpoint(group_losses)

    def total_losses(values):

        def advance(running, batch_block):
            part_loss, part_rows = checked(values, batch_block[0], batch_block[1], batch_block[2], batch_block[3], batch_block[4], pass_widths)
            return (running + part_loss, part_rows)
        summed, rows_all = lax.scan(advance, jnp.zeros((2,), jnp.float32), blocks)
        return (summed, rows_all)
    losses, pull_back, rows_all = jax.vjp(total_losses, params, has_aux=True)
    row_losses = jnp.transpose(rows_all, (1, 0, 2)).reshape(2, SEQS, L)
    all_grads = pull_back(jnp.ones((2,), jnp.float32))[0]
    squares = jnp.float32(0.0)
    for grad_item in all_grads:
        squares = squares + jnp.sum(grad_item * grad_item)
    grad_norm = jnp.sqrt(squares)
    clip_scale = clip_limit / jnp.maximum(grad_norm, clip_limit)
    attn_grad, norm_grad, up_grad, down_grad, embed_grad = [clip_scale * grad_item for grad_item in all_grads]
    attn_new, attn_m_new, attn_v_new = adamw(attn_master, attn_m, attn_v, attn_grad, rate_matrix)
    norm_new, norm_m_new, norm_v_new = adamw(norm_params, norm_m, norm_v, norm_grad, rate_gains)
    up_new, up_m_new, up_v_new = adamw(up_master, up_m, up_v, up_grad, rate_matrix)
    down_new, down_m_new, down_v_new = adamw(down_master, down_m, down_v, down_grad, rate_matrix)
    embed_new, embed_m_new, embed_v_new = adamw(embed_master, embed_m, embed_v, embed_grad, rate_matrix)
    ema_new = ema_decay * ema_old + (1.0 - ema_decay) * embed_new
    return (losses, row_losses, grad_norm.reshape(1), attn_new, attn_m_new, attn_v_new, norm_new, norm_m_new, norm_v_new, up_new, up_m_new, up_v_new, down_new, down_m_new, down_v_new, embed_new, embed_m_new, embed_v_new, ema_new, attn_new.astype(jnp.bfloat16), up_new.astype(jnp.bfloat16), down_new.astype(jnp.bfloat16), embed_new.astype(jnp.bfloat16))
```

```python
import math

import functools

import jax
import jax.numpy as jnp
import numpy as np
from jax import lax
from jax.experimental import pallas as pl
from jax.experimental.pallas import tpu as pltpu
from jax.sharding import PartitionSpec as P

HEADS = 8
HEAD = 64
V = 32768


smooth = 0.1
norm_eps = 1e-05
clip_limit = 0.005
beta_first = 0.9
beta_second = 0.98
adam_eps = 1e-08
rate_matrix = 0.02
rate_gains = 0.2
decay_weight = 0.01
ema_decay = 0.8
norm_count = 7


def merged(part, axis):
    gathered = lax.all_gather(jnp.stack(part), axis)
    row_peak = jnp.max(gathered[:, 0], axis=0)
    row_total = jnp.sum(gathered[:, 1] * jnp.exp(gathered[:, 0] - row_peak), axis=0)
    return row_peak, row_total, jnp.sum(gathered[:, 2], axis=0), jnp.sum(gathered[:, 3], axis=0)


def dot_rows(left, right):
    return lax.dot_general(
        left, right, (((1,), (1,)), ((), ())), preferred_element_type=jnp.float32
    )


def dot_cols(left, right):
    return lax.dot_general(
        left, right, (((0,), (0,)), ((), ())), preferred_element_type=jnp.float32
    )


def sinusoid(length, model_width):
    places = np.arange(length, dtype=np.float64)[:, None]
    halves = np.arange(model_width // 2, dtype=np.float64)[None, :]
    angles = places * np.exp(halves * (-2.0 * math.log(10000.0) / model_width))
    return jnp.asarray(np.concatenate([np.sin(angles), np.cos(angles)], axis=1), jnp.float32)


def layer_norm(values, gain, shift):
    centered = values - jnp.mean(values, axis=-1, keepdims=True)
    inverse = lax.rsqrt(jnp.mean(centered * centered, axis=-1, keepdims=True) + norm_eps)
    normed = centered * inverse
    return (normed * gain + shift, (normed, inverse))


def norm_back(upstream, stats, gain):
    normed, inverse = stats
    scaled = upstream * gain
    back = inverse * (
        scaled
        - jnp.mean(scaled, axis=-1, keepdims=True)
        - normed * jnp.mean(scaled * normed, axis=-1, keepdims=True)
    )
    return (back, jnp.sum(upstream * normed, axis=0), jnp.sum(upstream, axis=0))


def masked_scores(queries, key_rows, allowed):
    scores = jnp.einsum(
        "sqhe,skhe->shqk", queries, key_rows, preferred_element_type=jnp.float32
    ) * HEAD ** (-0.5)
    return jnp.where(allowed, scores, -1e30)


def attn_forward(q_in, kv_in, block, allowed, seq_dev):
    tokens = q_in.shape[0]
    width = block.shape[1] // 4
    queries = jnp.dot(q_in, block[:, :width], preferred_element_type=jnp.float32).astype(
        jnp.bfloat16
    )
    queries = queries.reshape(seq_dev, -1, HEADS, HEAD)
    pair = jnp.dot(kv_in, block[:, width : 3 * width], preferred_element_type=jnp.float32).astype(
        jnp.bfloat16
    )
    key_rows = pair[:, :width].reshape(seq_dev, -1, HEADS, HEAD)
    value_rows = pair[:, width:].reshape(seq_dev, -1, HEADS, HEAD)
    scores = masked_scores(queries, key_rows, allowed)
    row_peak = jnp.max(scores, axis=-1, keepdims=True)
    row_exp = jnp.exp(scores - row_peak)
    row_total = jnp.sum(row_exp, axis=-1, keepdims=True)
    log_total = row_peak + jnp.log(row_total)
    probs_low = (row_exp / row_total).astype(jnp.bfloat16)
    mixed_low = jnp.einsum(
        "shqk,skhe->sqhe", probs_low, value_rows, preferred_element_type=jnp.float32
    )
    mixed_low = mixed_low.reshape(tokens, width).astype(jnp.bfloat16)
    output = dot_rows(mixed_low, block[:, 3 * width :])
    return (output, (q_in, kv_in, queries, key_rows, value_rows, log_total, mixed_low, allowed))


def attention_backward_pass(kept, grad_low, block):
    q_in, kv_in, queries, key_rows, value_rows, log_total, mixed_low, allowed = kept
    tokens = q_in.shape[0]
    width = block.shape[1] // 4
    out_weight_grad = dot_cols(grad_low, mixed_low)
    mixed_grad = jnp.dot(
        grad_low, block[:, 3 * width :], preferred_element_type=jnp.float32
    ).astype(jnp.bfloat16)
    mixed_grad = mixed_grad.reshape(queries.shape)
    probs = jnp.exp(masked_scores(queries, key_rows, allowed) - log_total)
    probs_grad = jnp.einsum(
        "sqhe,skhe->shqk", mixed_grad, value_rows, preferred_element_type=jnp.float32
    )
    value_grad = jnp.einsum(
        "shqk,sqhe->skhe",
        probs.astype(jnp.bfloat16),
        mixed_grad,
        preferred_element_type=jnp.float32,
    )
    score_low = (probs * (probs_grad - jnp.sum(probs * probs_grad, axis=-1, keepdims=True))).astype(
        jnp.bfloat16
    )
    query_grad = jnp.einsum(
        "shqk,skhe->sqhe", score_low, key_rows, preferred_element_type=jnp.float32
    ) * HEAD ** (-0.5)
    key_grad = jnp.einsum(
        "shqk,sqhe->skhe", score_low, queries, preferred_element_type=jnp.float32
    ) * HEAD ** (-0.5)
    query_low = query_grad.reshape(tokens, width).astype(jnp.bfloat16)
    pair_low = jnp.concatenate(
        [key_grad.reshape(tokens, width), value_grad.reshape(tokens, width)], axis=1
    ).astype(jnp.bfloat16)
    block_grad = (dot_cols(q_in, query_low), dot_cols(kv_in, pair_low), out_weight_grad)
    return (
        dot_rows(query_low, block[:, :width]),
        dot_rows(pair_low, block[:, width : 3 * width]),
        block_grad,
    )


def ffn_pass(hidden, inner, down, width_now):
    inner = inner[:, : down.shape[0]]
    units = jnp.arange(inner.shape[1])[None, :]
    active = (units < width_now) & (inner > 0)
    act_low = jnp.where(active, inner, 0.0).astype(jnp.bfloat16)
    return (hidden + jnp.dot(act_low, down, preferred_element_type=jnp.float32), active, act_low)


def head_stats_kernel(block, offset_ref, table_ref, z_ref, target_ref, exp_ref, stat_ref):
    tile, rows = exp_ref.shape
    first = offset_ref[0] + pl.program_id(0) * tile
    ids = first + lax.broadcasted_iota(jnp.int32, (tile, block), 0)

    def step(index, carry):
        at = pl.ds(pl.multiple_of(index * block, block), block)
        logits = dot_rows(table_ref[...], z_ref[at, :])
        peak = jnp.max(logits, axis=0, keepdims=True)
        grown = jnp.exp(logits - peak)
        exp_ref[:, at] = grown.astype(jnp.bfloat16)
        hits = ids == target_ref[:, at]
        stat_ref[0, 0:1, at] = peak
        stat_ref[0, 1:2, at] = jnp.sum(grown, axis=0, keepdims=True)
        stat_ref[0, 2:3, at] = jnp.sum(jnp.where(hits, logits, 0.0), axis=0, keepdims=True)
        stat_ref[0, 3:4, at] = jnp.sum(logits, axis=0, keepdims=True)
        return carry

    lax.fori_loop(0, rows // block, step, 0, unroll=4)


def head_stats(head_in, row_targets, table_part, offset):
    rows, width = head_in.shape
    vocab = table_part.shape[0]
    tile, block = math.gcd(vocab, 512), math.gcd(rows, 512)
    tiles = vocab // tile
    exps, stats = pl.pallas_call(
        functools.partial(head_stats_kernel, block),
        out_shape=(
            jax.ShapeDtypeStruct((vocab, rows), jnp.bfloat16),
            jax.ShapeDtypeStruct((tiles, 4, rows), jnp.float32),
        ),
        grid_spec=pltpu.PrefetchScalarGridSpec(
            num_scalar_prefetch=1,
            grid=(tiles,),
            in_specs=[
                pl.BlockSpec((tile, width), lambda t, o: (t, 0)),
                pl.BlockSpec((rows, width), lambda t, o: (0, 0), pipeline_mode=pl.Buffered(1)),
                pl.BlockSpec((1, rows), lambda t, o: (0, 0)),
            ],
            out_specs=(
                pl.BlockSpec((tile, rows), lambda t, o: (t, 0)),
                pl.BlockSpec((1, 4, rows), lambda t, o: (t, 0, 0)),
            ),
        ),
        compiler_params=pltpu.CompilerParams(vmem_limit_bytes=56 << 20),
        name="head_stats",
    )(offset.reshape(1), table_part, head_in, row_targets.reshape(1, rows))
    return exps, stats


def head_grads_kernel(
    block, offset_ref, exp_ref, table_t_ref, z_ref, target_ref, weight_ref, scale_ref, dz_ref,
    dtable_ref, acc_ref,
):
    tile, rows = exp_ref.shape
    t = pl.program_id(0)
    last = pl.num_programs(0) - 1
    first = offset_ref[0] + t * tile
    ids = first + lax.broadcasted_iota(jnp.int32, (tile, block), 0)

    def step(index, carry):
        at = pl.ds(pl.multiple_of(index * block, block), block)
        weight = weight_ref[:, at]
        hits = ids == target_ref[:, at]
        grad = exp_ref[:, at].astype(jnp.float32) * scale_ref[0, :, at] - jnp.where(
            hits, weight * (1.0 - smooth + smooth / V), weight * (smooth / V)
        )
        low = grad.astype(jnp.bfloat16)
        part = jnp.dot(low, z_ref[at, :], preferred_element_type=jnp.float32)
        dtable_ref[...] = jnp.where(index == 0, part, dtable_ref[...] + part)
        back = jnp.dot(table_t_ref[...], low, preferred_element_type=jnp.float32)
        total = jnp.where(t == 0, back, acc_ref[index] + back)
        acc_ref[index] = total

        @pl.when(t == last)
        def _():
            dz_ref[at, :] = total.T.astype(jnp.bfloat16)

        return carry

    lax.fori_loop(0, rows // block, step, 0)


def head_grads(head_in, row_targets, row_weights, scale, exps, table_t, offset):
    rows, width = head_in.shape
    vocab = exps.shape[0]
    tile, block = math.gcd(vocab, 512), math.gcd(rows, 1024)
    tiles = vocab // tile
    row = pl.BlockSpec((1, rows), lambda t, o: (0, 0))
    return pl.pallas_call(
        functools.partial(head_grads_kernel, block),
        out_shape=(
            jax.ShapeDtypeStruct((rows, width), jnp.bfloat16),
            jax.ShapeDtypeStruct((vocab, width), jnp.float32),
        ),
        grid_spec=pltpu.PrefetchScalarGridSpec(
            num_scalar_prefetch=1,
            grid=(tiles,),
            in_specs=[
                pl.BlockSpec((tile, rows), lambda t, o: (t, 0)),
                pl.BlockSpec((width, tile), lambda t, o: (0, t)),
                pl.BlockSpec((rows, width), lambda t, o: (0, 0), pipeline_mode=pl.Buffered(1)),
                row,
                row,
                pl.BlockSpec((1, 1, rows), lambda t, o: (t, 0, 0)),
            ],
            out_specs=(
                pl.BlockSpec((rows, width), lambda t, o: (0, 0), pipeline_mode=pl.Buffered(1)),
                pl.BlockSpec((tile, width), lambda t, o: (t, 0)),
            ),
            scratch_shapes=[pltpu.VMEM((rows // block, width, block), jnp.float32)],
        ),
        compiler_params=pltpu.CompilerParams(vmem_limit_bytes=60 << 20),
        name="head_grads",
    )(
        offset.reshape(1), exps, table_t, head_in, row_targets.reshape(1, rows),
        row_weights.reshape(1, rows), scale,
    )


def adamw(weight, first_m, second_m, grad_item, step_rate):
    first_new = beta_first * first_m + (1.0 - beta_first) * grad_item
    second_new = beta_second * second_m + (1.0 - beta_second) * grad_item * grad_item
    weight_new = weight - step_rate * (
        first_new / (jnp.sqrt(second_new) + adam_eps) + decay_weight * weight
    )
    return (weight_new, first_new, second_new)


def rows_of(source, row_start, number):
    return lax.dynamic_slice_in_dim(source, row_start, number, 0).reshape(-1)


def local(
    source_ids,
    token_ids,
    targets,
    pad_mask,
    pass_widths,
    attn_master,
    attn_m,
    attn_v,
    norm_params,
    norm_m,
    norm_v,
    up_master,
    up_m,
    up_v,
    down_master,
    down_m,
    down_v,
    embed_master,
    embed_m,
    embed_v,
    ema_old,
):
    wide_count = lax.axis_size("wide")
    wide_at = lax.axis_index("wide")
    dp_count = lax.axis_size("dp")
    dp_at = lax.axis_index("dp")
    model_width = norm_params.shape[1]
    length = token_ids.shape[1]
    seq_dev = token_ids.shape[0] // (wide_count * dp_count)
    tokens = seq_dev * length
    vocab_shard = embed_master.shape[0]
    attn_full = lax.all_gather(attn_master.astype(jnp.bfloat16), ("dp", "wide"), axis=1, tiled=True)
    up_full, down_full = (
        lax.all_gather(up_master.astype(jnp.bfloat16), "wide", axis=2, tiled=True),
        lax.all_gather(down_master.astype(jnp.bfloat16), "wide", axis=1, tiled=True),
    )
    table_local = embed_master.astype(jnp.bfloat16)
    group_start = dp_at * wide_count * seq_dev
    own_start = group_start + wide_at * seq_dev
    count_all = jnp.sum(pad_mask).astype(jnp.float32)
    group_src = rows_of(source_ids, group_start, wide_count * seq_dev).reshape(wide_count, tokens)
    group_tgt = rows_of(token_ids, group_start, wide_count * seq_dev).reshape(wide_count, tokens)
    group_ids = jnp.concatenate([group_src, group_tgt], axis=1).reshape(-1)
    own_mask = rows_of(pad_mask, own_start, seq_dev).reshape(seq_dev, length) > 0
    free_mask = own_mask[:, None, None, :]
    causal = jnp.arange(length)[:, None] >= jnp.arange(length)[None, :]
    causal_mask = free_mask & causal[None, None]
    offset = wide_at * vocab_shard
    picked = group_ids - offset
    inside = (picked >= 0) & (picked < vocab_shard)
    found_rows = jnp.take(table_local, jnp.clip(picked, 0, vocab_shard - 1), axis=0).astype(
        jnp.float32
    )
    embedded = lax.psum_scatter(
        jnp.where(inside[:, None], found_rows, 0.0).astype(jnp.bfloat16),
        "wide",
        scatter_dimension=0,
        tiled=True,
    ).astype(jnp.float32)
    position = jnp.tile(sinusoid(length, model_width), (seq_dev, 1))
    src_in = math.sqrt(model_width) * embedded[:tokens] + position
    tgt_in = math.sqrt(model_width) * embedded[tokens:] + position

    def norm_at(values, index):
        return layer_norm(values, norm_params[index], norm_params[norm_count + index])

    src_val, source_norm_statistics = norm_at(src_in, 0)
    src_low = src_val.astype(jnp.bfloat16)
    src_att, src_kept = attn_forward(src_low, src_low, attn_full[0], free_mask, seq_dev)
    src_hidden = src_in + src_att
    sff_val, sff_stats = norm_at(src_hidden, 1)
    sff_low = sff_val.astype(jnp.bfloat16)
    src_inner = jnp.dot(sff_low, up_full[0], preferred_element_type=jnp.float32)
    tgt_val, tgt_stats = norm_at(tgt_in, 3)
    tgt_low = tgt_val.astype(jnp.bfloat16)
    tgt_att, tgt_kept = attn_forward(tgt_low, tgt_low, attn_full[1], causal_mask, seq_dev)
    tgt_hidden = tgt_in + tgt_att
    cross_val, cross_stats = norm_at(tgt_hidden, 4)
    cross_low = cross_val.astype(jnp.bfloat16)
    passes = []
    final_list = []
    pass_units = (up_full.shape[2], up_full.shape[2] // 2)
    for pass_index in range(2):
        held = pass_units[pass_index]
        enc_out, enc_active, enc_act = ffn_pass(
            src_hidden, src_inner, down_full[0, :held], pass_widths[pass_index]
        )
        mem_val, mem_stats = norm_at(enc_out, 2)
        mem_low = mem_val.astype(jnp.bfloat16)
        x_att, x_kept = attn_forward(cross_low, mem_low, attn_full[2], free_mask, seq_dev)
        crossed = tgt_hidden + x_att
        dff_val, dff_stats = norm_at(crossed, 5)
        dff_low = dff_val.astype(jnp.bfloat16)
        dec_inner = jnp.dot(dff_low, up_full[1, :, :held], preferred_element_type=jnp.float32)
        dec_out, dec_active, dec_act = ffn_pass(
            crossed, dec_inner, down_full[1, :held], pass_widths[pass_index]
        )
        fin_val, fin_stats = norm_at(dec_out, 6)
        passes.append(
            (
                enc_active,
                enc_act,
                mem_stats,
                x_kept,
                dff_stats,
                dff_low,
                dec_active,
                dec_act,
                fin_stats,
            )
        )
        final_list.append(fin_val.astype(jnp.bfloat16))
    final_pair = (final_list[0], final_list[1])
    gathered = (
        lax.all_gather(final_pair[0], "wide", axis=0, tiled=True),
        lax.all_gather(final_pair[1], "wide", axis=0, tiled=True),
    )
    head_in = jnp.concatenate(gathered, axis=0)
    row_targets = jnp.tile(rows_of(targets, group_start, wide_count * seq_dev), 2)
    row_masks = jnp.tile(
        rows_of(pad_mask, group_start, wide_count * seq_dev).astype(jnp.float32), 2
    )
    chunk = math.gcd(head_in.shape[0], 4096)
    chunks = [slice(at, at + chunk) for at in range(0, head_in.shape[0], chunk)]
    exps, stats = zip(
        *[head_stats(head_in[at], row_targets[at], table_local, offset) for at in chunks]
    )
    stats = jnp.concatenate(stats, axis=2)
    tile_peaks = stats[:, 0]
    own_peak = jnp.max(tile_peaks, axis=0)
    own_total = jnp.sum(stats[:, 1] * jnp.exp(tile_peaks - own_peak), axis=0)
    row_peak, row_total, target_logit, logit_sum = merged(
        (own_peak, own_total, jnp.sum(stats[:, 2], axis=0), jnp.sum(stats[:, 3], axis=0)), "wide"
    )
    row_weights = row_masks / count_all
    log_total = row_peak + jnp.log(row_total)
    row_error = log_total - (1.0 - smooth) * target_logit - smooth / V * logit_sum
    row_loss = (row_weights * row_error).reshape(2, -1)
    row_plain = (row_masks * row_error).reshape(2, -1)
    scale = (row_weights * jnp.exp(tile_peaks - log_total))[:, None, :]
    row_grads, table_grad = zip(
        *[
            head_grads(
                head_in[at], row_targets[at], row_weights[at], scale[:, :, at], part,
                table_local.T, offset,
            )
            for at, part in zip(chunks, exps)
        ]
    )
    row_grads, table_grad = jnp.concatenate(row_grads), sum(table_grad)
    half_rows = head_in.shape[0] // 2
    loss_own = jnp.sum(lax.dynamic_slice_in_dim(row_loss, wide_at * tokens, tokens, 1), axis=1)
    plain_own = lax.dynamic_slice_in_dim(row_plain, wide_at * tokens, tokens, 1)
    final_grads = (
        lax.psum_scatter(
            row_grads[:half_rows], "wide", scatter_dimension=0, tiled=True
        ).astype(jnp.float32),
        lax.psum_scatter(
            row_grads[half_rows:], "wide", scatter_dimension=0, tiled=True
        ).astype(jnp.float32),
    )
    row_losses = plain_own.reshape(2, seq_dev, length)
    gain_parts = [jnp.zeros((model_width,), jnp.float32) for index in range(norm_count)]
    shift_parts = [jnp.zeros((model_width,), jnp.float32) for index in range(norm_count)]

    def backward_layer_norm(upstream, stats, index):
        back, gain_part, shift_part = norm_back(upstream, stats, norm_params[index])
        gain_parts[index] = gain_parts[index] + gain_part
        shift_parts[index] = shift_parts[index] + shift_part
        return back

    src_inner_grad = jnp.zeros(src_inner.shape, jnp.float32)
    source_hidden_gradient = jnp.zeros((tokens, model_width), jnp.float32)
    tgt_hidden_grad = jnp.zeros((tokens, model_width), jnp.float32)
    cross_grad = jnp.zeros((tokens, model_width), jnp.float32)
    cross_weight = []
    up_grads = [[], []]
    down_grads = [[], []]
    for pass_index in range(2):
        (
            enc_active,
            enc_act,
            mem_stats,
            x_kept,
            dff_stats,
            dff_low,
            dec_active,
            dec_act,
            fin_stats,
        ) = passes[pass_index]
        out_grad = backward_layer_norm(final_grads[pass_index], fin_stats, 6)
        out_low = out_grad.astype(jnp.bfloat16)
        held = pass_units[pass_index]
        down_grads[1].append(dot_cols(dec_act, out_low))
        dec_low = jnp.where(
            dec_active, dot_rows(out_low, down_full[1, :held]), 0.0
        ).astype(jnp.bfloat16)
        up_grads[1].append(dot_cols(dec_low, dff_low))
        crossed_grad = out_grad + backward_layer_norm(
            dot_rows(dec_low, up_full[1, :, :held]), dff_stats, 5
        )
        query_in, memory_in, block_grad = attention_backward_pass(
            x_kept, crossed_grad.astype(jnp.bfloat16), attn_full[2]
        )
        cross_weight.append(block_grad)
        tgt_hidden_grad = tgt_hidden_grad + crossed_grad
        cross_grad = cross_grad + query_in
        enc_grad = backward_layer_norm(memory_in, mem_stats, 2)
        enc_low = enc_grad.astype(jnp.bfloat16)
        down_grads[0].append(dot_cols(enc_act, enc_low))
        src_inner_grad = src_inner_grad + jnp.pad(
            jnp.where(enc_active, dot_rows(enc_low, down_full[0, :held]), 0.0),
            ((0, 0), (0, src_inner.shape[1] - held)),
        )
        source_hidden_gradient = source_hidden_gradient + enc_grad
    tgt_hidden_grad = tgt_hidden_grad + backward_layer_norm(cross_grad, cross_stats, 4)
    src_inner_low = src_inner_grad.astype(jnp.bfloat16)
    up_grads[0].append(dot_cols(src_inner_low, sff_low))
    source_hidden_gradient = source_hidden_gradient + backward_layer_norm(
        dot_rows(src_inner_low, up_full[0]), sff_stats, 1
    )
    tq_in, tkv_in, tgt_weight = attention_backward_pass(
        tgt_kept, tgt_hidden_grad.astype(jnp.bfloat16), attn_full[1]
    )
    tgt_in_grad = tgt_hidden_grad + backward_layer_norm(tq_in + tkv_in, tgt_stats, 3)
    source_query_input, source_key_value_input, source_norm_weight = attention_backward_pass(
        src_kept, source_hidden_gradient.astype(jnp.bfloat16), attn_full[0]
    )
    source_input_gradient = source_hidden_gradient + backward_layer_norm(
        source_query_input + source_key_value_input, source_norm_statistics, 0
    )
    def joined(parts):
        whole, *rest = parts
        if rest:
            half = rest[0].shape[0]
            whole = jnp.concatenate([whole[:half] + rest[0], whole[half:]])
        return whole

    def scattered(parts):
        return lax.psum_scatter(joined(parts), "wide", scatter_dimension=0, tiled=True)

    hidden_shard = jnp.stack(
        [scattered(parts) for parts in (down_grads[1], up_grads[1], down_grads[0], up_grads[0])]
    )
    cross_pair = tuple(first + second for first, second in zip(*cross_weight))
    shards = dp_count * wide_count
    attn_grad = jnp.stack(
        [
            jnp.concatenate(list(block), axis=1).reshape(
                shards, -1, 128
            )
            for block in (source_norm_weight, tgt_weight, cross_pair)
        ],
        axis=1,
    )
    norm_grad = jnp.stack(gain_parts + shift_parts)
    embed_low = (
        math.sqrt(model_width) * jnp.concatenate([source_input_gradient, tgt_in_grad], axis=0)
    ).astype(jnp.bfloat16)
    spread_rows = lax.all_gather(embed_low, "wide", axis=0, tiled=True)
    local_ids = group_ids - offset
    inside_rows = (local_ids >= 0) & (local_ids < vocab_shard)
    embed_part = table_grad.at[jnp.clip(local_ids, 0, vocab_shard - 1)].add(
        jnp.where(inside_rows[:, None], spread_rows.astype(jnp.float32), 0.0)
    )
    attn_shard = (
        lax.psum_scatter(
            lax.psum_scatter(
                attn_grad.reshape(-1, 128), "dp", scatter_dimension=0, tiled=True
            ),
            "wide",
            scatter_dimension=0,
            tiled=True,
        )
        .reshape(attn_master.shape)
        .astype(jnp.float32)
    )
    hidden_sum = lax.psum(hidden_shard, "dp")
    embed_sum = lax.psum(embed_part.astype(jnp.bfloat16), "dp").astype(jnp.float32)
    down_sum = jnp.stack([hidden_sum[2], hidden_sum[0]])
    up_sum = jnp.stack([hidden_sum[3].T, hidden_sum[1].T])
    square_part = (
        jnp.sum(attn_shard * attn_shard)
        + (jnp.sum(up_sum * up_sum) + jnp.sum(down_sum * down_sum) + jnp.sum(embed_sum * embed_sum))
        / dp_count
    )
    square_all, norm_sum, losses = lax.psum((square_part, norm_grad, loss_own), ("dp", "wide"))
    grad_norm = jnp.sqrt(square_all + jnp.sum(norm_sum * norm_sum))
    clip_scale = clip_limit / jnp.maximum(grad_norm, clip_limit)
    attn_new, attn_m_new, attn_v_new = adamw(
        attn_master, attn_m, attn_v, clip_scale * attn_shard, rate_matrix
    )
    norm_new, norm_m_new, norm_v_new = adamw(
        norm_params, norm_m, norm_v, clip_scale * norm_sum, rate_gains
    )
    up_new, up_m_new, up_v_new = adamw(up_master, up_m, up_v, clip_scale * up_sum, rate_matrix)
    down_new, down_m_new, down_v_new = adamw(
        down_master, down_m, down_v, clip_scale * down_sum, rate_matrix
    )
    embed_new, embed_m_new, embed_v_new = adamw(
        embed_master, embed_m, embed_v, clip_scale * embed_sum, rate_matrix
    )
    ema_cols = ema_old.shape[1]
    ema_new = ema_decay * ema_old + (1.0 - ema_decay) * lax.dynamic_slice_in_dim(
        embed_new, dp_at * ema_cols, ema_cols, 1
    )
    return (
        losses,
        row_losses,
        grad_norm.reshape(1),
        attn_new,
        attn_m_new,
        attn_v_new,
        norm_new,
        norm_m_new,
        norm_v_new,
        up_new,
        up_m_new,
        up_v_new,
        down_new,
        down_m_new,
        down_v_new,
        embed_new,
        embed_m_new,
        embed_v_new,
        ema_new,
        attn_new.astype(jnp.bfloat16),
        up_new.astype(jnp.bfloat16),
        down_new.astype(jnp.bfloat16),
        embed_new.astype(jnp.bfloat16),
    )


def solution(mesh):
    in_specs = (
        P(),
        P(),
        P(),
        P(),
        P(),
        P(None, ("dp", "wide"), None),
        P(None, ("dp", "wide"), None),
        P(None, ("dp", "wide"), None),
        P(),
        P(),
        P(),
        P(None, None, "wide"),
        P(None, None, "wide"),
        P(None, None, "wide"),
        P(None, "wide", None),
        P(None, "wide", None),
        P(None, "wide", None),
        P("wide", None),
        P("wide", None),
        P("wide", None),
        P("wide", "dp"),
    )
    out_specs = (
        P(),
        P(None, ("dp", "wide"), None),
        P(),
        P(None, ("dp", "wide"), None),
        P(None, ("dp", "wide"), None),
        P(None, ("dp", "wide"), None),
        P(),
        P(),
        P(),
        P(None, None, "wide"),
        P(None, None, "wide"),
        P(None, None, "wide"),
        P(None, "wide", None),
        P(None, "wide", None),
        P(None, "wide", None),
        P("wide", None),
        P("wide", None),
        P("wide", None),
        P("wide", "dp"),
        P(None, ("dp", "wide"), None),
        P(None, None, "wide"),
        P(None, "wide", None),
        P("wide", None),
    )
    return jax.shard_map(local, mesh=mesh, in_specs=in_specs, out_specs=out_specs, check_vma=False)
```

```python
import math

import functools

import jax
import jax.numpy as jnp
import numpy as np
from jax import lax
from jax.experimental import pallas as pl
from jax.experimental.pallas import tpu as pltpu
from jax.sharding import PartitionSpec as P

HEADS = 8
HEAD = 64
V = 32768


MESH = pl.DeviceIdType.MESH
smooth = 0.1
norm_eps = 1e-05
clip_limit = 0.005
beta_first = 0.9
beta_second = 0.98
adam_eps = 1e-08
rate_matrix = 0.02
rate_gains = 0.2
decay_weight = 0.01
ema_decay = 0.8
norm_count = 7


def merged(part, axis):
    gathered = lax.all_gather(jnp.stack(part), axis)
    row_peak = jnp.max(gathered[:, 0], axis=0)
    row_total = jnp.sum(gathered[:, 1] * jnp.exp(gathered[:, 0] - row_peak), axis=0)
    return row_peak, row_total, jnp.sum(gathered[:, 2], axis=0), jnp.sum(gathered[:, 3], axis=0)


def dot_rows(left, right):
    return lax.dot_general(
        left, right, (((1,), (1,)), ((), ())), preferred_element_type=jnp.float32
    )


def dot_cols(left, right):
    return lax.dot_general(
        left, right, (((0,), (0,)), ((), ())), preferred_element_type=jnp.float32
    )


def sinusoid(length, model_width):
    places = np.arange(length, dtype=np.float64)[:, None]
    halves = np.arange(model_width // 2, dtype=np.float64)[None, :]
    angles = places * np.exp(halves * (-2.0 * math.log(10000.0) / model_width))
    return jnp.asarray(np.concatenate([np.sin(angles), np.cos(angles)], axis=1), jnp.float32)


def layer_norm(values, gain, shift):
    centered = values - jnp.mean(values, axis=-1, keepdims=True)
    inverse = lax.rsqrt(jnp.mean(centered * centered, axis=-1, keepdims=True) + norm_eps)
    normed = centered * inverse
    return (normed * gain + shift, (normed, inverse))


def norm_back(upstream, stats, gain):
    normed, inverse = stats
    scaled = upstream * gain
    back = inverse * (
        scaled
        - jnp.mean(scaled, axis=-1, keepdims=True)
        - normed * jnp.mean(scaled * normed, axis=-1, keepdims=True)
    )
    return (back, jnp.sum(upstream * normed, axis=0), jnp.sum(upstream, axis=0))


def masked_scores(queries, key_rows, allowed):
    scores = jnp.einsum(
        "sqhe,skhe->shqk", queries, key_rows, preferred_element_type=jnp.float32
    ) * HEAD ** (-0.5)
    return jnp.where(allowed, scores, -1e30)


def attn_forward(q_in, kv_in, block, allowed, seq_dev):
    tokens = q_in.shape[0]
    width = block.shape[1] // 4
    queries = jnp.dot(q_in, block[:, :width], preferred_element_type=jnp.float32).astype(
        jnp.bfloat16
    )
    queries = queries.reshape(seq_dev, -1, HEADS, HEAD)
    pair = jnp.dot(kv_in, block[:, width : 3 * width], preferred_element_type=jnp.float32).astype(
        jnp.bfloat16
    )
    key_rows = pair[:, :width].reshape(seq_dev, -1, HEADS, HEAD)
    value_rows = pair[:, width:].reshape(seq_dev, -1, HEADS, HEAD)
    scores = masked_scores(queries, key_rows, allowed)
    row_peak = jnp.max(scores, axis=-1, keepdims=True)
    row_exp = jnp.exp(scores - row_peak)
    row_total = jnp.sum(row_exp, axis=-1, keepdims=True)
    log_total = row_peak + jnp.log(row_total)
    probs_low = (row_exp / row_total).astype(jnp.bfloat16)
    mixed_low = jnp.einsum(
        "shqk,skhe->sqhe", probs_low, value_rows, preferred_element_type=jnp.float32
    )
    mixed_low = mixed_low.reshape(tokens, width).astype(jnp.bfloat16)
    output = dot_rows(mixed_low, block[:, 3 * width :])
    return (output, (q_in, kv_in, queries, key_rows, value_rows, log_total, mixed_low, allowed))


def attention_backward_pass(kept, grad_low, block):
    q_in, kv_in, queries, key_rows, value_rows, log_total, mixed_low, allowed = kept
    tokens = q_in.shape[0]
    width = block.shape[1] // 4
    out_weight_grad = dot_cols(grad_low, mixed_low)
    mixed_grad = jnp.dot(
        grad_low, block[:, 3 * width :], preferred_element_type=jnp.float32
    ).astype(jnp.bfloat16)
    mixed_grad = mixed_grad.reshape(queries.shape)
    probs = jnp.exp(masked_scores(queries, key_rows, allowed) - log_total)
    probs_grad = jnp.einsum(
        "sqhe,skhe->shqk", mixed_grad, value_rows, preferred_element_type=jnp.float32
    )
    value_grad = jnp.einsum(
        "shqk,sqhe->skhe",
        probs.astype(jnp.bfloat16),
        mixed_grad,
        preferred_element_type=jnp.float32,
    )
    score_low = (probs * (probs_grad - jnp.sum(probs * probs_grad, axis=-1, keepdims=True))).astype(
        jnp.bfloat16
    )
    query_grad = jnp.einsum(
        "shqk,skhe->sqhe", score_low, key_rows, preferred_element_type=jnp.float32
    ) * HEAD ** (-0.5)
    key_grad = jnp.einsum(
        "shqk,sqhe->skhe", score_low, queries, preferred_element_type=jnp.float32
    ) * HEAD ** (-0.5)
    query_low = query_grad.reshape(tokens, width).astype(jnp.bfloat16)
    pair_low = jnp.concatenate(
        [key_grad.reshape(tokens, width), value_grad.reshape(tokens, width)], axis=1
    ).astype(jnp.bfloat16)
    block_grad = (dot_cols(q_in, query_low), dot_cols(kv_in, pair_low), out_weight_grad)
    return (
        dot_rows(query_low, block[:, :width]),
        dot_rows(pair_low, block[:, width : 3 * width]),
        block_grad,
    )


def ffn_pass(hidden, inner, down, width_now):
    inner = inner[:, : down.shape[0]]
    units = jnp.arange(inner.shape[1])[None, :]
    active = (units < width_now) & (inner > 0)
    act_low = jnp.where(active, inner, 0.0).astype(jnp.bfloat16)
    return (hidden + jnp.dot(act_low, down, preferred_element_type=jnp.float32), active, act_low)


def head_stats_kernel(block, offset_ref, table_ref, z_ref, target_ref, exp_ref, stat_ref):
    tile, rows = exp_ref.shape
    first = offset_ref[0] + pl.program_id(0) * tile
    ids = first + lax.broadcasted_iota(jnp.int32, (tile, block), 0)

    def step(index, carry):
        at = pl.ds(pl.multiple_of(index * block, block), block)
        logits = dot_rows(table_ref[...], z_ref[at, :])
        peak = jnp.max(logits, axis=0, keepdims=True)
        grown = jnp.exp(logits - peak)
        exp_ref[:, at] = grown.astype(jnp.bfloat16)
        hits = ids == target_ref[:, at]
        stat_ref[0, 0:1, at] = peak
        stat_ref[0, 1:2, at] = jnp.sum(grown, axis=0, keepdims=True)
        stat_ref[0, 2:3, at] = jnp.sum(jnp.where(hits, logits, 0.0), axis=0, keepdims=True)
        stat_ref[0, 3:4, at] = jnp.sum(logits, axis=0, keepdims=True)
        return carry

    lax.fori_loop(0, rows // block, step, 0, unroll=4)


def head_stats(head_in, row_targets, table_part, offset):
    rows, width = head_in.shape
    vocab = table_part.shape[0]
    tile, block = math.gcd(vocab, 512), math.gcd(rows, 512)
    tiles = vocab // tile
    exps, stats = pl.pallas_call(
        functools.partial(head_stats_kernel, block),
        out_shape=(
            jax.ShapeDtypeStruct((vocab, rows), jnp.bfloat16),
            jax.ShapeDtypeStruct((tiles, 4, rows), jnp.float32),
        ),
        grid_spec=pltpu.PrefetchScalarGridSpec(
            num_scalar_prefetch=1,
            grid=(tiles,),
            in_specs=[
                pl.BlockSpec((tile, width), lambda t, o: (t, 0)),
                pl.BlockSpec((rows, width), lambda t, o: (0, 0), pipeline_mode=pl.Buffered(1)),
                pl.BlockSpec((1, rows), lambda t, o: (0, 0)),
            ],
            out_specs=(
                pl.BlockSpec((tile, rows), lambda t, o: (t, 0)),
                pl.BlockSpec((1, 4, rows), lambda t, o: (t, 0, 0)),
            ),
        ),
        compiler_params=pltpu.CompilerParams(vmem_limit_bytes=56 << 20),
        name="head_stats",
    )(offset.reshape(1), table_part, head_in, row_targets.reshape(1, rows))
    return exps, stats


def head_grads_kernel(
    block, offset_ref, exp_ref, table_t_ref, z_ref, target_ref, weight_ref, scale_ref, dz_ref,
    dtable_ref, acc_ref,
):
    tile, rows = exp_ref.shape
    t = pl.program_id(0)
    last = pl.num_programs(0) - 1
    first = offset_ref[0] + t * tile
    ids = first + lax.broadcasted_iota(jnp.int32, (tile, block), 0)

    def step(index, carry):
        at = pl.ds(pl.multiple_of(index * block, block), block)
        weight = weight_ref[:, at]
        hits = ids == target_ref[:, at]
        grad = exp_ref[:, at].astype(jnp.float32) * scale_ref[0, :, at] - jnp.where(
            hits, weight * (1.0 - smooth + smooth / V), weight * (smooth / V)
        )
        low = grad.astype(jnp.bfloat16)
        part = jnp.dot(low, z_ref[at, :], preferred_element_type=jnp.float32)
        dtable_ref[...] = jnp.where(index == 0, part, dtable_ref[...] + part)
        back = jnp.dot(table_t_ref[...], low, preferred_element_type=jnp.float32)
        total = jnp.where(t == 0, back, acc_ref[index] + back)
        acc_ref[index] = total

        @pl.when(t == last)
        def _():
            dz_ref[at, :] = total.T.astype(jnp.bfloat16)

        return carry

    lax.fori_loop(0, rows // block, step, 0)


def head_grads(head_in, row_targets, row_weights, scale, exps, table_t, offset):
    rows, width = head_in.shape
    vocab = exps.shape[0]
    tile, block = math.gcd(vocab, 512), math.gcd(rows, 1024)
    tiles = vocab // tile
    row = pl.BlockSpec((1, rows), lambda t, o: (0, 0))
    return pl.pallas_call(
        functools.partial(head_grads_kernel, block),
        out_shape=(
            jax.ShapeDtypeStruct((rows, width), jnp.bfloat16),
            jax.ShapeDtypeStruct((vocab, width), jnp.float32),
        ),
        grid_spec=pltpu.PrefetchScalarGridSpec(
            num_scalar_prefetch=1,
            grid=(tiles,),
            in_specs=[
                pl.BlockSpec((tile, rows), lambda t, o: (t, 0)),
                pl.BlockSpec((width, tile), lambda t, o: (0, t)),
                pl.BlockSpec((rows, width), lambda t, o: (0, 0), pipeline_mode=pl.Buffered(1)),
                row,
                row,
                pl.BlockSpec((1, 1, rows), lambda t, o: (t, 0, 0)),
            ],
            out_specs=(
                pl.BlockSpec((rows, width), lambda t, o: (0, 0), pipeline_mode=pl.Buffered(1)),
                pl.BlockSpec((tile, width), lambda t, o: (t, 0)),
            ),
            scratch_shapes=[pltpu.VMEM((rows // block, width, block), jnp.float32)],
        ),
        compiler_params=pltpu.CompilerParams(vmem_limit_bytes=60 << 20),
        name="head_grads",
    )(
        offset.reshape(1), exps, table_t, head_in, row_targets.reshape(1, rows),
        row_weights.reshape(1, rows), scale,
    )


def reduce_kernel(*refs):
    hidden, attn, (hidden_out, attn_out) = refs[:4], refs[4], refs[5:7]
    own_f, own_a, sib_f, sib_a, plane_f, plane_a, far_f, far_a = refs[7:15]
    load_sem, pair_send, pair_recv, plane_send, plane_recv, far_send, far_recv = refs[15:]
    f32 = jnp.float32
    dp, wide = lax.axis_index("dp"), lax.axis_index("wide")
    level, core = wide // 2, wide % 2
    sibling = (dp, level * 2 + 1 - core)
    row, col = dp // 2, dp % 2
    peers = (row * 2 + 1 - col, (1 - row) * 2 + col, (1 - row) * 2 + 1 - col)
    far = [lax.rem(level + 1 + j, 4) for j in range(4)]

    barrier = pltpu.get_barrier_semaphore()
    partners = [sibling] + [(p, wide) for p in peers] + [(dp, far[j] * 2 + core) for j in range(3)]
    for device in partners:
        pl.semaphore_signal(barrier, inc=1, device_id=device, device_id_type=MESH)
    pl.semaphore_wait(barrier, len(partners))

    def remote(src, dst, send, recv, device):
        copy = pltpu.make_async_remote_copy(
            src_ref=src, dst_ref=dst, send_sem=send, recv_sem=recv, device_id=device, device_id_type=MESH
        )
        copy.start()
        return copy

    pair, loads = [], []
    for j in range(4):
        mine, theirs = far[j] * 2 + core, far[j] * 2 + 1 - core
        for k in range(4):
            pair.append(
                remote(hidden[k].at[theirs], sib_f.at[j, k], pair_send.at[j, k], pair_recv.at[j, k], sibling)
            )
            load = pltpu.make_async_copy(hidden[k].at[mine], own_f.at[j, k], load_sem.at[j, k])
            load.start()
            loads.append(load)
        pair.append(
            remote(attn.at[:, theirs], sib_a.at[j], pair_send.at[j, 4], pair_recv.at[j, 4], sibling)
        )
        load = pltpu.make_async_copy(attn.at[:, mine], own_a.at[j], load_sem.at[j, 4])
        load.start()
        loads.append(load)

    plane = []
    for j in range(4):
        for index in range(5):
            loads[5 * j + index].wait()
            pair[5 * j + index].wait_recv()

        def add_f(k, carry):
            for q in range(4):
                own_f[j, k, q] = (own_f[j, k, q].astype(f32) + sib_f[j, k, q].astype(f32)).astype(jnp.bfloat16)
            return carry

        lax.fori_loop(0, 4, add_f, 0)

        def add_a(q, carry):
            own_a[j, q] = (own_a[j, q].astype(f32) + sib_a[j, q].astype(f32)).astype(jnp.bfloat16)
            return carry

        lax.fori_loop(0, 4, add_a, 0)
        sent = []
        for p, peer in enumerate(peers):
            sent.append(
                (
                    remote(own_f.at[j, :, peer], plane_f.at[j, p], plane_send.at[j, p, 0], plane_recv.at[j, p, 0], (peer, wide)),
                    remote(own_a.at[j, peer], plane_a.at[j, p], plane_send.at[j, p, 1], plane_recv.at[j, p, 1], (peer, wide)),
                )
            )
        plane.append(sent)

    flown = []
    for j in range(4):
        for sent in plane[j]:
            for copy in sent:
                copy.wait_recv()

        def total_f(k):
            total = own_f[j, k, dp].astype(f32)
            for p in range(3):
                total += plane_f[j, p, k].astype(f32)
            return total

        def total_a():
            total = own_a[j, dp].astype(f32)
            for p in range(3):
                total += plane_a[j, p].astype(f32)
            return total

        if j < 3:

            def keep(k, carry):
                plane_f[j, 0, k] = total_f(k).astype(jnp.bfloat16)
                return carry

            lax.fori_loop(0, 4, keep, 0)
            plane_a[j, 0] = total_a().astype(jnp.bfloat16)
            device = (dp, far[j] * 2 + core)
            flown.append(
                (
                    remote(plane_f.at[j, 0], far_f.at[j], far_send.at[j, 0], far_recv.at[j, 0], device),
                    remote(plane_a.at[j, 0], far_a.at[j], far_send.at[j, 1], far_recv.at[j, 1], device),
                )
            )
        else:

            def last(k, carry):
                hidden_out[k] = total_f(k)
                return carry

            lax.fori_loop(0, 4, last, 0)
            attn_out[...] = total_a()
    for j in range(3):
        for copy in flown[j]:
            copy.wait_recv()

        def finish(k, carry):
            hidden_out[k] += far_f[j, k].astype(f32)
            return carry

        lax.fori_loop(0, 4, finish, 0)
        attn_out[...] += far_a[j].astype(f32)
    for copy in pair:
        copy.wait_send()
    for sent in plane:
        for both in sent:
            for copy in both:
                copy.wait_send()
    for both in flown:
        for copy in both:
            copy.wait_send()


def reduced(hidden, attn, cid):
    _, _, rows, width = hidden[0].shape
    lines = attn.shape[2]
    bf = jnp.bfloat16
    hbm = pl.BlockSpec(memory_space=pltpu.HBM)
    vmem = pl.BlockSpec(memory_space=pltpu.VMEM)
    dma = pltpu.SemaphoreType.DMA
    return pl.pallas_call(
        reduce_kernel,
        out_shape=(
            jax.ShapeDtypeStruct((4, rows, width), jnp.float32),
            jax.ShapeDtypeStruct((lines, 128), jnp.float32),
        ),
        in_specs=[hbm] * 5,
        out_specs=(vmem, vmem),
        scratch_shapes=[
            pltpu.VMEM((4, 4, 4, rows, width), bf),
            pltpu.VMEM((4, 4, lines, 128), bf),
            pltpu.VMEM((4, 4, 4, rows, width), bf),
            pltpu.VMEM((4, 4, lines, 128), bf),
            pltpu.VMEM((4, 3, 4, rows, width), bf),
            pltpu.VMEM((4, 3, lines, 128), bf),
            pltpu.VMEM((3, 4, rows, width), bf),
            pltpu.VMEM((3, lines, 128), bf),
            dma((4, 5)), dma((4, 5)), dma((4, 5)), dma((4, 3, 2)), dma((4, 3, 2)), dma((3, 2)), dma((3, 2)),
        ],
        compiler_params=pltpu.CompilerParams(collective_id=cid, has_side_effects=True, vmem_limit_bytes=56 << 20),
        name="reduce_grads",
    )(*hidden, attn)


def adamw(weight, first_m, second_m, grad_item, step_rate):
    first_new = beta_first * first_m + (1.0 - beta_first) * grad_item
    second_new = beta_second * second_m + (1.0 - beta_second) * grad_item * grad_item
    weight_new = weight - step_rate * (
        first_new / (jnp.sqrt(second_new) + adam_eps) + decay_weight * weight
    )
    return (weight_new, first_new, second_new)


def rows_of(source, row_start, number):
    return lax.dynamic_slice_in_dim(source, row_start, number, 0).reshape(-1)


def local(
    source_ids,
    token_ids,
    targets,
    pad_mask,
    pass_widths,
    attn_master,
    attn_m,
    attn_v,
    norm_params,
    norm_m,
    norm_v,
    up_master,
    up_m,
    up_v,
    down_master,
    down_m,
    down_v,
    embed_master,
    embed_m,
    embed_v,
    ema_old,
):
    wide_count = lax.axis_size("wide")
    wide_at = lax.axis_index("wide")
    dp_count = lax.axis_size("dp")
    dp_at = lax.axis_index("dp")
    model_width = norm_params.shape[1]
    length = token_ids.shape[1]
    seq_dev = token_ids.shape[0] // (wide_count * dp_count)
    tokens = seq_dev * length
    vocab_shard = embed_master.shape[0]
    planes = (dp_count, wide_count) == (4, 8)
    link_type = jnp.bfloat16 if planes else jnp.float32
    attn_full = lax.all_gather(attn_master.astype(jnp.bfloat16), ("dp", "wide"), axis=1, tiled=True)
    up_full, down_full = (
        lax.all_gather(up_master.astype(jnp.bfloat16), "wide", axis=2, tiled=True),
        lax.all_gather(down_master.astype(jnp.bfloat16), "wide", axis=1, tiled=True),
    )
    table_local = embed_master.astype(jnp.bfloat16)
    group_start = dp_at * wide_count * seq_dev
    own_start = group_start + wide_at * seq_dev
    count_all = jnp.sum(pad_mask).astype(jnp.float32)
    group_src = rows_of(source_ids, group_start, wide_count * seq_dev).reshape(wide_count, tokens)
    group_tgt = rows_of(token_ids, group_start, wide_count * seq_dev).reshape(wide_count, tokens)
    group_ids = jnp.concatenate([group_src, group_tgt], axis=1).reshape(-1)
    own_mask = rows_of(pad_mask, own_start, seq_dev).reshape(seq_dev, length) > 0
    free_mask = own_mask[:, None, None, :]
    causal = jnp.arange(length)[:, None] >= jnp.arange(length)[None, :]
    causal_mask = free_mask & causal[None, None]
    offset = wide_at * vocab_shard
    picked = group_ids - offset
    inside = (picked >= 0) & (picked < vocab_shard)
    found_rows = jnp.take(table_local, jnp.clip(picked, 0, vocab_shard - 1), axis=0).astype(
        jnp.float32
    )
    embedded = lax.psum_scatter(
        jnp.where(inside[:, None], found_rows, 0.0).astype(jnp.bfloat16),
        "wide",
        scatter_dimension=0,
        tiled=True,
    ).astype(jnp.float32)
    position = jnp.tile(sinusoid(length, model_width), (seq_dev, 1))
    src_in = math.sqrt(model_width) * embedded[:tokens] + position
    tgt_in = math.sqrt(model_width) * embedded[tokens:] + position

    def norm_at(values, index):
        return layer_norm(values, norm_params[index], norm_params[norm_count + index])

    src_val, source_norm_statistics = norm_at(src_in, 0)
    src_low = src_val.astype(jnp.bfloat16)
    src_att, src_kept = attn_forward(src_low, src_low, attn_full[0], free_mask, seq_dev)
    src_hidden = src_in + src_att
    sff_val, sff_stats = norm_at(src_hidden, 1)
    sff_low = sff_val.astype(jnp.bfloat16)
    src_inner = jnp.dot(sff_low, up_full[0], preferred_element_type=jnp.float32)
    tgt_val, tgt_stats = norm_at(tgt_in, 3)
    tgt_low = tgt_val.astype(jnp.bfloat16)
    tgt_att, tgt_kept = attn_forward(tgt_low, tgt_low, attn_full[1], causal_mask, seq_dev)
    tgt_hidden = tgt_in + tgt_att
    cross_val, cross_stats = norm_at(tgt_hidden, 4)
    cross_low = cross_val.astype(jnp.bfloat16)
    passes = []
    final_list = []
    pass_units = (up_full.shape[2], up_full.shape[2] // 2)
    for pass_index in range(2):
        held = pass_units[pass_index]
        enc_out, enc_active, enc_act = ffn_pass(
            src_hidden, src_inner, down_full[0, :held], pass_widths[pass_index]
        )
        mem_val, mem_stats = norm_at(enc_out, 2)
        mem_low = mem_val.astype(jnp.bfloat16)
        x_att, x_kept = attn_forward(cross_low, mem_low, attn_full[2], free_mask, seq_dev)
        crossed = tgt_hidden + x_att
        dff_val, dff_stats = norm_at(crossed, 5)
        dff_low = dff_val.astype(jnp.bfloat16)
        dec_inner = jnp.dot(dff_low, up_full[1, :, :held], preferred_element_type=jnp.float32)
        dec_out, dec_active, dec_act = ffn_pass(
            crossed, dec_inner, down_full[1, :held], pass_widths[pass_index]
        )
        fin_val, fin_stats = norm_at(dec_out, 6)
        passes.append(
            (
                enc_active,
                enc_act,
                mem_stats,
                x_kept,
                dff_stats,
                dff_low,
                dec_active,
                dec_act,
                fin_stats,
            )
        )
        final_list.append(fin_val.astype(jnp.bfloat16))
    final_pair = (final_list[0], final_list[1])
    gathered = (
        lax.all_gather(final_pair[0], "wide", axis=0, tiled=True),
        lax.all_gather(final_pair[1], "wide", axis=0, tiled=True),
    )
    head_in = jnp.concatenate(gathered, axis=0)
    row_targets = jnp.tile(rows_of(targets, group_start, wide_count * seq_dev), 2)
    row_masks = jnp.tile(
        rows_of(pad_mask, group_start, wide_count * seq_dev).astype(jnp.float32), 2
    )
    chunk = math.gcd(head_in.shape[0], 4096)
    chunks = [slice(at, at + chunk) for at in range(0, head_in.shape[0], chunk)]
    exps, stats = zip(
        *[head_stats(head_in[at], row_targets[at], table_local, offset) for at in chunks]
    )
    stats = jnp.concatenate(stats, axis=2)
    tile_peaks = stats[:, 0]
    own_peak = jnp.max(tile_peaks, axis=0)
    own_total = jnp.sum(stats[:, 1] * jnp.exp(tile_peaks - own_peak), axis=0)
    row_peak, row_total, target_logit, logit_sum = merged(
        (own_peak, own_total, jnp.sum(stats[:, 2], axis=0), jnp.sum(stats[:, 3], axis=0)), "wide"
    )
    row_weights = row_masks / count_all
    log_total = row_peak + jnp.log(row_total)
    row_error = log_total - (1.0 - smooth) * target_logit - smooth / V * logit_sum
    row_loss = (row_weights * row_error).reshape(2, -1)
    row_plain = (row_masks * row_error).reshape(2, -1)
    scale = (row_weights * jnp.exp(tile_peaks - log_total))[:, None, :]
    row_grads, table_grad = zip(
        *[
            head_grads(
                head_in[at], row_targets[at], row_weights[at], scale[:, :, at], part,
                table_local.T, offset,
            )
            for at, part in zip(chunks, exps)
        ]
    )
    row_grads, table_grad = jnp.concatenate(row_grads), sum(table_grad)
    half_rows = head_in.shape[0] // 2
    loss_own = jnp.sum(lax.dynamic_slice_in_dim(row_loss, wide_at * tokens, tokens, 1), axis=1)
    plain_own = lax.dynamic_slice_in_dim(row_plain, wide_at * tokens, tokens, 1)
    final_grads = (
        lax.psum_scatter(
            row_grads[:half_rows], "wide", scatter_dimension=0, tiled=True
        ).astype(jnp.float32),
        lax.psum_scatter(
            row_grads[half_rows:], "wide", scatter_dimension=0, tiled=True
        ).astype(jnp.float32),
    )
    row_losses = plain_own.reshape(2, seq_dev, length)
    gain_parts = [jnp.zeros((model_width,), jnp.float32) for index in range(norm_count)]
    shift_parts = [jnp.zeros((model_width,), jnp.float32) for index in range(norm_count)]

    def backward_layer_norm(upstream, stats, index):
        back, gain_part, shift_part = norm_back(upstream, stats, norm_params[index])
        gain_parts[index] = gain_parts[index] + gain_part
        shift_parts[index] = shift_parts[index] + shift_part
        return back

    src_inner_grad = jnp.zeros(src_inner.shape, jnp.float32)
    source_hidden_gradient = jnp.zeros((tokens, model_width), jnp.float32)
    tgt_hidden_grad = jnp.zeros((tokens, model_width), jnp.float32)
    cross_grad = jnp.zeros((tokens, model_width), jnp.float32)
    cross_weight = []
    up_grads = [[], []]
    down_grads = [[], []]
    for pass_index in range(2):
        (
            enc_active,
            enc_act,
            mem_stats,
            x_kept,
            dff_stats,
            dff_low,
            dec_active,
            dec_act,
            fin_stats,
        ) = passes[pass_index]
        out_grad = backward_layer_norm(final_grads[pass_index], fin_stats, 6)
        out_low = out_grad.astype(jnp.bfloat16)
        held = pass_units[pass_index]
        down_grads[1].append(dot_cols(dec_act, out_low))
        dec_low = jnp.where(
            dec_active, dot_rows(out_low, down_full[1, :held]), 0.0
        ).astype(jnp.bfloat16)
        up_grads[1].append(dot_cols(dec_low, dff_low))
        crossed_grad = out_grad + backward_layer_norm(
            dot_rows(dec_low, up_full[1, :, :held]), dff_stats, 5
        )
        query_in, memory_in, block_grad = attention_backward_pass(
            x_kept, crossed_grad.astype(jnp.bfloat16), attn_full[2]
        )
        cross_weight.append(block_grad)
        tgt_hidden_grad = tgt_hidden_grad + crossed_grad
        cross_grad = cross_grad + query_in
        enc_grad = backward_layer_norm(memory_in, mem_stats, 2)
        enc_low = enc_grad.astype(jnp.bfloat16)
        down_grads[0].append(dot_cols(enc_act, enc_low))
        src_inner_grad = src_inner_grad + jnp.pad(
            jnp.where(enc_active, dot_rows(enc_low, down_full[0, :held]), 0.0),
            ((0, 0), (0, src_inner.shape[1] - held)),
        )
        source_hidden_gradient = source_hidden_gradient + enc_grad
    tgt_hidden_grad = tgt_hidden_grad + backward_layer_norm(cross_grad, cross_stats, 4)
    src_inner_low = src_inner_grad.astype(jnp.bfloat16)
    up_grads[0].append(dot_cols(src_inner_low, sff_low))
    source_hidden_gradient = source_hidden_gradient + backward_layer_norm(
        dot_rows(src_inner_low, up_full[0]), sff_stats, 1
    )
    tq_in, tkv_in, tgt_weight = attention_backward_pass(
        tgt_kept, tgt_hidden_grad.astype(jnp.bfloat16), attn_full[1]
    )
    tgt_in_grad = tgt_hidden_grad + backward_layer_norm(tq_in + tkv_in, tgt_stats, 3)
    source_query_input, source_key_value_input, source_norm_weight = attention_backward_pass(
        src_kept, source_hidden_gradient.astype(jnp.bfloat16), attn_full[0]
    )
    source_input_gradient = source_hidden_gradient + backward_layer_norm(
        source_query_input + source_key_value_input, source_norm_statistics, 0
    )
    def joined(parts):
        whole, *rest = parts
        if rest:
            half = rest[0].shape[0]
            whole = jnp.concatenate([whole[:half] + rest[0], whole[half:]])
        return whole

    hidden_grads = [joined(p) for p in (down_grads[1], up_grads[1], down_grads[0], up_grads[0])]
    cross_pair = tuple(first + second for first, second in zip(*cross_weight))
    shards = dp_count * wide_count
    attn_grad = jnp.stack(
        [
            jnp.concatenate(block, axis=1).astype(link_type).reshape(shards, -1, 128)
            for block in (source_norm_weight, tgt_weight, cross_pair)
        ],
        axis=1,
    )
    norm_grad = jnp.stack(gain_parts + shift_parts)
    embed_low = (
        math.sqrt(model_width) * jnp.concatenate([source_input_gradient, tgt_in_grad], axis=0)
    ).astype(jnp.bfloat16)
    spread_rows = lax.all_gather(embed_low, "wide", axis=0, tiled=True)
    local_ids = group_ids - offset
    inside_rows = (local_ids >= 0) & (local_ids < vocab_shard)
    embed_part = table_grad.at[jnp.clip(local_ids, 0, vocab_shard - 1)].add(
        jnp.where(inside_rows[:, None], spread_rows.astype(jnp.float32), 0.0)
    )
    if planes:
        hidden_part, attn_shard = reduced(
            [
                part.astype(link_type).reshape(wide_count, dp_count, -1, model_width)
                for part in hidden_grads
            ],
            attn_grad.reshape(dp_count, wide_count, -1, 128),
            1,
        )
        hidden_sum = jnp.moveaxis(
            lax.all_gather(hidden_part.astype(link_type), "dp"), 0, 1
        ).reshape(4, -1, model_width).astype(jnp.float32)
        square_part = jnp.sum(hidden_part * hidden_part)
    else:
        hidden_sum = lax.psum(
            jnp.stack(
                [
                    lax.psum_scatter(part, "wide", scatter_dimension=0, tiled=True)
                    for part in hidden_grads
                ]
            ),
            "dp",
        )
        square_part = jnp.sum(hidden_sum * hidden_sum) / dp_count
        attn_shard = lax.psum_scatter(
            lax.psum_scatter(
                attn_grad.reshape(-1, 128), "dp", scatter_dimension=0, tiled=True
            ),
            "wide",
            scatter_dimension=0,
            tiled=True,
        )
    attn_shard = attn_shard.reshape(attn_master.shape)
    embed_sum = lax.psum(embed_part.astype(jnp.bfloat16), "dp").astype(jnp.float32)
    down_sum = jnp.stack([hidden_sum[2], hidden_sum[0]])
    up_sum = jnp.stack([hidden_sum[3].T, hidden_sum[1].T])
    square_part += (
        jnp.sum(attn_shard * attn_shard) + jnp.sum(embed_sum * embed_sum) / dp_count
    )
    square_all, norm_sum, losses = lax.psum((square_part, norm_grad, loss_own), ("dp", "wide"))
    grad_norm = jnp.sqrt(square_all + jnp.sum(norm_sum * norm_sum))
    clip_scale = clip_limit / jnp.maximum(grad_norm, clip_limit)
    attn_new, attn_m_new, attn_v_new = adamw(
        attn_master, attn_m, attn_v, clip_scale * attn_shard, rate_matrix
    )
    norm_new, norm_m_new, norm_v_new = adamw(
        norm_params, norm_m, norm_v, clip_scale * norm_sum, rate_gains
    )
    up_new, up_m_new, up_v_new = adamw(up_master, up_m, up_v, clip_scale * up_sum, rate_matrix)
    down_new, down_m_new, down_v_new = adamw(
        down_master, down_m, down_v, clip_scale * down_sum, rate_matrix
    )
    embed_new, embed_m_new, embed_v_new = adamw(
        embed_master, embed_m, embed_v, clip_scale * embed_sum, rate_matrix
    )
    ema_cols = ema_old.shape[1]
    ema_new = ema_decay * ema_old + (1.0 - ema_decay) * lax.dynamic_slice_in_dim(
        embed_new, dp_at * ema_cols, ema_cols, 1
    )
    return (
        losses,
        row_losses,
        grad_norm.reshape(1),
        attn_new,
        attn_m_new,
        attn_v_new,
        norm_new,
        norm_m_new,
        norm_v_new,
        up_new,
        up_m_new,
        up_v_new,
        down_new,
        down_m_new,
        down_v_new,
        embed_new,
        embed_m_new,
        embed_v_new,
        ema_new,
        attn_new.astype(jnp.bfloat16),
        up_new.astype(jnp.bfloat16),
        down_new.astype(jnp.bfloat16),
        embed_new.astype(jnp.bfloat16),
    )


def solution(mesh):
    in_specs = (
        P(),
        P(),
        P(),
        P(),
        P(),
        P(None, ("dp", "wide"), None),
        P(None, ("dp", "wide"), None),
        P(None, ("dp", "wide"), None),
        P(),
        P(),
        P(),
        P(None, None, "wide"),
        P(None, None, "wide"),
        P(None, None, "wide"),
        P(None, "wide", None),
        P(None, "wide", None),
        P(None, "wide", None),
        P("wide", None),
        P("wide", None),
        P("wide", None),
        P("wide", "dp"),
    )
    out_specs = (
        P(),
        P(None, ("dp", "wide"), None),
        P(),
        P(None, ("dp", "wide"), None),
        P(None, ("dp", "wide"), None),
        P(None, ("dp", "wide"), None),
        P(),
        P(),
        P(),
        P(None, None, "wide"),
        P(None, None, "wide"),
        P(None, None, "wide"),
        P(None, "wide", None),
        P(None, "wide", None),
        P(None, "wide", None),
        P("wide", None),
        P("wide", None),
        P("wide", None),
        P("wide", "dp"),
        P(None, ("dp", "wide"), None),
        P(None, None, "wide"),
        P(None, "wide", None),
        P("wide", None),
    )
    return jax.shard_map(local, mesh=mesh, in_specs=in_specs, out_specs=out_specs, check_vma=False)
```

```python
import math

import functools

import jax
import jax.numpy as jnp
import numpy as np
from jax import lax
from jax.experimental import pallas as pl
from jax.experimental.pallas import tpu as pltpu
from jax.sharding import PartitionSpec as P

HEADS = 8
HEAD = 64
V = 32768


MESH = pl.DeviceIdType.MESH
smooth = 0.1
norm_eps = 1e-05
clip_limit = 0.005
beta_first = 0.9
beta_second = 0.98
adam_eps = 1e-08
rate_matrix = 0.02
rate_gains = 0.2
decay_weight = 0.01
ema_decay = 0.8
norm_count = 7


def merged(part, axis):
    gathered = lax.all_gather(jnp.stack(part), axis)
    row_peak = jnp.max(gathered[:, 0], axis=0)
    row_total = jnp.sum(gathered[:, 1] * jnp.exp(gathered[:, 0] - row_peak), axis=0)
    return row_peak, row_total, jnp.sum(gathered[:, 2], axis=0), jnp.sum(gathered[:, 3], axis=0)


def dot_rows(left, right):
    return lax.dot_general(
        left, right, (((1,), (1,)), ((), ())), preferred_element_type=jnp.float32
    )


def dot_cols(left, right):
    return lax.dot_general(
        left, right, (((0,), (0,)), ((), ())), preferred_element_type=jnp.float32
    )


def sinusoid(length, model_width):
    places = np.arange(length, dtype=np.float64)[:, None]
    halves = np.arange(model_width // 2, dtype=np.float64)[None, :]
    angles = places * np.exp(halves * (-2.0 * math.log(10000.0) / model_width))
    return jnp.asarray(np.concatenate([np.sin(angles), np.cos(angles)], axis=1), jnp.float32)


def layer_norm(values, gain, shift):
    centered = values - jnp.mean(values, axis=-1, keepdims=True)
    inverse = lax.rsqrt(jnp.mean(centered * centered, axis=-1, keepdims=True) + norm_eps)
    normed = centered * inverse
    return (normed * gain + shift, (normed, inverse))


def norm_back(upstream, stats, gain):
    normed, inverse = stats
    scaled = upstream * gain
    back = inverse * (
        scaled
        - jnp.mean(scaled, axis=-1, keepdims=True)
        - normed * jnp.mean(scaled * normed, axis=-1, keepdims=True)
    )
    return (back, jnp.sum(upstream * normed, axis=0), jnp.sum(upstream, axis=0))


def masked_scores(queries, key_rows, allowed):
    scores = jnp.einsum(
        "sqhe,skhe->shqk", queries, key_rows, preferred_element_type=jnp.float32
    ) * HEAD ** (-0.5)
    return jnp.where(allowed, scores, -1e30)


def attn_forward(q_in, kv_in, block, allowed, seq_dev):
    tokens = q_in.shape[0]
    width = block.shape[1] // 4
    queries = jnp.dot(q_in, block[:, :width], preferred_element_type=jnp.float32).astype(
        jnp.bfloat16
    )
    queries = queries.reshape(seq_dev, -1, HEADS, HEAD)
    pair = jnp.dot(kv_in, block[:, width : 3 * width], preferred_element_type=jnp.float32).astype(
        jnp.bfloat16
    )
    key_rows = pair[:, :width].reshape(seq_dev, -1, HEADS, HEAD)
    value_rows = pair[:, width:].reshape(seq_dev, -1, HEADS, HEAD)
    scores = masked_scores(queries, key_rows, allowed)
    row_peak = jnp.max(scores, axis=-1, keepdims=True)
    row_exp = jnp.exp(scores - row_peak)
    row_total = jnp.sum(row_exp, axis=-1, keepdims=True)
    log_total = row_peak + jnp.log(row_total)
    probs_low = (row_exp / row_total).astype(jnp.bfloat16)
    mixed_low = jnp.einsum(
        "shqk,skhe->sqhe", probs_low, value_rows, preferred_element_type=jnp.float32
    )
    mixed_low = mixed_low.reshape(tokens, width).astype(jnp.bfloat16)
    output = dot_rows(mixed_low, block[:, 3 * width :])
    return (output, (q_in, kv_in, queries, key_rows, value_rows, log_total, mixed_low, allowed))


def attention_backward_pass(kept, grad_low, block):
    q_in, kv_in, queries, key_rows, value_rows, log_total, mixed_low, allowed = kept
    tokens = q_in.shape[0]
    width = block.shape[1] // 4
    mixed_grad = jnp.dot(
        grad_low, block[:, 3 * width :], preferred_element_type=jnp.float32
    ).astype(jnp.bfloat16)
    mixed_grad = mixed_grad.reshape(queries.shape)
    probs = jnp.exp(masked_scores(queries, key_rows, allowed) - log_total)
    probs_grad = jnp.einsum(
        "sqhe,skhe->shqk", mixed_grad, value_rows, preferred_element_type=jnp.float32
    )
    value_grad = jnp.einsum(
        "shqk,sqhe->skhe",
        probs.astype(jnp.bfloat16),
        mixed_grad,
        preferred_element_type=jnp.float32,
    )
    score_low = (probs * (probs_grad - jnp.sum(probs * probs_grad, axis=-1, keepdims=True))).astype(
        jnp.bfloat16
    )
    query_grad = jnp.einsum(
        "shqk,skhe->sqhe", score_low, key_rows, preferred_element_type=jnp.float32
    ) * HEAD ** (-0.5)
    key_grad = jnp.einsum(
        "shqk,sqhe->skhe", score_low, queries, preferred_element_type=jnp.float32
    ) * HEAD ** (-0.5)
    query_low = query_grad.reshape(tokens, width).astype(jnp.bfloat16)
    pair_low = jnp.concatenate(
        [key_grad.reshape(tokens, width), value_grad.reshape(tokens, width)], axis=1
    ).astype(jnp.bfloat16)
    return (
        dot_rows(query_low, block[:, :width]),
        dot_rows(pair_low, block[:, width : 3 * width]),
        (q_in, query_low, kv_in, pair_low, grad_low, mixed_low),
    )


def ffn_pass(hidden, inner, down, width_now):
    inner = inner[:, : down.shape[0]]
    units = jnp.arange(inner.shape[1])[None, :]
    active = (units < width_now) & (inner > 0)
    act_low = jnp.where(active, inner, 0.0).astype(jnp.bfloat16)
    return (hidden + jnp.dot(act_low, down, preferred_element_type=jnp.float32), active, act_low)


def head_stats_kernel(block, offset_ref, table_ref, z_ref, target_ref, exp_ref, stat_ref):
    tile, rows = exp_ref.shape
    first = offset_ref[0] + pl.program_id(0) * tile
    ids = first + lax.broadcasted_iota(jnp.int32, (tile, block), 0)

    def step(index, carry):
        at = pl.ds(pl.multiple_of(index * block, block), block)
        logits = dot_rows(table_ref[...], z_ref[at, :])
        peak = jnp.max(logits, axis=0, keepdims=True)
        grown = jnp.exp(logits - peak)
        exp_ref[:, at] = grown.astype(jnp.bfloat16)
        hits = ids == target_ref[:, at]
        stat_ref[0, 0:1, at] = peak
        stat_ref[0, 1:2, at] = jnp.sum(grown, axis=0, keepdims=True)
        stat_ref[0, 2:3, at] = jnp.sum(jnp.where(hits, logits, 0.0), axis=0, keepdims=True)
        stat_ref[0, 3:4, at] = jnp.sum(logits, axis=0, keepdims=True)
        return carry

    lax.fori_loop(0, rows // block, step, 0, unroll=4)


def head_stats(head_in, row_targets, table_part, offset):
    rows, width = head_in.shape
    vocab = table_part.shape[0]
    tile, block = math.gcd(vocab, 512), math.gcd(rows, 512)
    tiles = vocab // tile
    exps, stats = pl.pallas_call(
        functools.partial(head_stats_kernel, block),
        out_shape=(
            jax.ShapeDtypeStruct((vocab, rows), jnp.bfloat16),
            jax.ShapeDtypeStruct((tiles, 4, rows), jnp.float32),
        ),
        grid_spec=pltpu.PrefetchScalarGridSpec(
            num_scalar_prefetch=1,
            grid=(tiles,),
            in_specs=[
                pl.BlockSpec((tile, width), lambda t, o: (t, 0)),
                pl.BlockSpec((rows, width), lambda t, o: (0, 0), pipeline_mode=pl.Buffered(1)),
                pl.BlockSpec((1, rows), lambda t, o: (0, 0)),
            ],
            out_specs=(
                pl.BlockSpec((tile, rows), lambda t, o: (t, 0)),
                pl.BlockSpec((1, 4, rows), lambda t, o: (t, 0, 0)),
            ),
        ),
        compiler_params=pltpu.CompilerParams(vmem_limit_bytes=56 << 20),
        name="head_stats",
    )(offset.reshape(1), table_part, head_in, row_targets.reshape(1, rows))
    return exps, stats


def head_grads_kernel(
    block, offset_ref, exp_ref, table_t_ref, z_ref, target_ref, weight_ref, scale_ref, dz_ref,
    dtable_ref, acc_ref,
):
    tile, rows = exp_ref.shape
    t = pl.program_id(0)
    last = pl.num_programs(0) - 1
    first = offset_ref[0] + t * tile
    ids = first + lax.broadcasted_iota(jnp.int32, (tile, block), 0)

    def step(index, carry):
        at = pl.ds(pl.multiple_of(index * block, block), block)
        weight = weight_ref[:, at]
        hits = ids == target_ref[:, at]
        grad = exp_ref[:, at].astype(jnp.float32) * scale_ref[0, :, at] - jnp.where(
            hits, weight * (1.0 - smooth + smooth / V), weight * (smooth / V)
        )
        low = grad.astype(jnp.bfloat16)
        part = jnp.dot(low, z_ref[at, :], preferred_element_type=jnp.float32)
        dtable_ref[...] = jnp.where(index == 0, part, dtable_ref[...] + part)
        back = jnp.dot(table_t_ref[...], low, preferred_element_type=jnp.float32)
        total = jnp.where(t == 0, back, acc_ref[index] + back)
        acc_ref[index] = total

        @pl.when(t == last)
        def _():
            dz_ref[at, :] = total.T.astype(jnp.bfloat16)

        return carry

    lax.fori_loop(0, rows // block, step, 0)


def head_grads(head_in, row_targets, row_weights, scale, exps, table_t, offset):
    rows, width = head_in.shape
    vocab = exps.shape[0]
    tile, block = math.gcd(vocab, 512), math.gcd(rows, 1024)
    tiles = vocab // tile
    row = pl.BlockSpec((1, rows), lambda t, o: (0, 0))
    return pl.pallas_call(
        functools.partial(head_grads_kernel, block),
        out_shape=(
            jax.ShapeDtypeStruct((rows, width), jnp.bfloat16),
            jax.ShapeDtypeStruct((vocab, width), jnp.float32),
        ),
        grid_spec=pltpu.PrefetchScalarGridSpec(
            num_scalar_prefetch=1,
            grid=(tiles,),
            in_specs=[
                pl.BlockSpec((tile, rows), lambda t, o: (t, 0)),
                pl.BlockSpec((width, tile), lambda t, o: (0, t)),
                pl.BlockSpec((rows, width), lambda t, o: (0, 0), pipeline_mode=pl.Buffered(1)),
                row,
                row,
                pl.BlockSpec((1, 1, rows), lambda t, o: (t, 0, 0)),
            ],
            out_specs=(
                pl.BlockSpec((rows, width), lambda t, o: (0, 0), pipeline_mode=pl.Buffered(1)),
                pl.BlockSpec((tile, width), lambda t, o: (t, 0)),
            ),
            scratch_shapes=[pltpu.VMEM((rows // block, width, block), jnp.float32)],
        ),
        compiler_params=pltpu.CompilerParams(vmem_limit_bytes=60 << 20),
        name="head_grads",
    )(
        offset.reshape(1), exps, table_t, head_in, row_targets.reshape(1, rows),
        row_weights.reshape(1, rows), scale,
    )


def gather_kernel(
    f_shard, a_pair, f_full, a_full, local_sem, fz_send, fz_recv, fp_send, fp_recv, fs_send, fs_recv,
    az_send, az_recv, ap_send, ap_recv, as_send, as_recv,
):
    dp, wide = lax.axis_index("dp"), lax.axis_index("wide")
    level, core = wide // 2, wide % 2
    row, col = dp // 2, dp % 2
    sibling = (dp, level * 2 + 1 - core)
    beside, across = row * 2 + 1 - col, (1 - row) * 2 + col
    peers = (beside, across, (1 - row) * 2 + 1 - col)
    half = a_pair.shape[2]

    barrier = pltpu.get_barrier_semaphore()

    def greet(device):
        pl.semaphore_signal(barrier, inc=1, device_id=device, device_id_type=MESH)

    for device in [sibling] + [(p, wide) for p in peers]:
        greet(device)
    can = (level < 3, level > 0)
    step = (1, -1)
    for d in range(2):
        pl.when(can[d])(functools.partial(greet, (dp, (level + step[d]) * 2 + core)))
    pl.semaphore_wait(barrier, 4 + can[0].astype(jnp.int32) + can[1].astype(jnp.int32))

    def remote(src, dst, send, recv, device):
        return pltpu.make_async_remote_copy(
            src_ref=src, dst_ref=dst, send_sem=send, recv_sem=recv, device_id=device, device_id_type=MESH
        )

    def f_at(part, source):
        return f_full.at[pl.ds(2 * part, 2), source * 2 + core, (col, row)[part]]

    def f_other(part, source):
        return f_full.at[pl.ds(2 * part, 2), source * 2 + core, 1 - (col, row)[part]]

    def a_at(owner, source, side=core):
        return a_full.at[
            :, owner * 4 + source, :, pl.ds(pl.multiple_of(side * half, 128), half)
        ]

    def source_of(d, t):
        return level - step[d] * t

    def valid(d, t):
        return (level >= t, level <= 3 - t)[d]

    def chain_f(d, t, part):
        source = source_of(d, t)
        src = f_shard.at[pl.ds(2 * part, 2), (col, row)[part]] if t == 0 else f_at(part, source)
        device = (dp, (level + step[d]) * 2 + core)
        return remote(src, f_at(part, source), fz_send.at[d, t, part], fz_recv.at[d, t, part], device)

    def chain_a(d, t):
        source = source_of(d, t)
        src = a_pair if t == 0 else a_at(dp, source)
        device = (dp, (level + step[d]) * 2 + core)
        return remote(src, a_at(dp, source), az_send.at[d, t], az_recv.at[d, t], device)

    def chain(d, t):
        return [chain_a(d, t), chain_f(d, t, 0), chain_f(d, t, 1)]

    def plane_f(d, t, part):
        at = f_at(part, source_of(d, t))
        device = ((beside, across)[part], wide)
        return remote(at, at, fp_send.at[d, t - 1, part], fp_recv.at[d, t - 1, part], device)

    def plane_a(d, t, slot, p):
        source = source_of(d, t)
        src = a_pair if t == 0 else a_at(dp, source)
        return remote(src, a_at(dp, source), ap_send.at[slot, p], ap_recv.at[slot, p], (peers[p], wide))

    def pair_f(d, t, slot, other, part):
        at = (f_other if other else f_at)(part, source_of(d, t))
        return remote(at, at, fs_send.at[slot, other, part], fs_recv.at[slot, other, part], sibling)

    def pair_a(owner, d, t, slot, p):
        source = source_of(d, t)
        src = a_pair if (t == 0 and p == 3) else a_at(owner, source)
        return remote(src, a_at(owner, source), as_send.at[slot, p], as_recv.at[slot, p], sibling)

    items = [(d, t) for t in (1, 2, 3) for d in range(2)]

    def slot_of(d, t):
        return 1 + 2 * (t - 1) + d

    def start(copies):
        for copy in copies:
            copy.start()

    for d in range(2):
        pl.when(can[d])(lambda d=d: start(chain(d, 0)))
    own = [
        pltpu.make_async_copy(f_shard, f_full.at[:, wide], local_sem.at[0]),
        pltpu.make_async_copy(a_pair, a_at(dp, level), local_sem.at[1]),
    ]
    start(own)
    start([plane_a(0, 0, 0, p) for p in range(3)])
    own_pair = [
        remote(f_shard, f_full.at[:, wide], fs_send.at[0, 0, 0], fs_recv.at[0, 0, 0], sibling),
        pair_a(dp, 0, 0, 0, 3),
    ]
    start(own_pair)

    for d, t in items:

        def arrived(d=d, t=t):
            chain_a(d, t - 1).wait_recv()
            if t < 3:
                pl.when(can[d])(lambda: chain_a(d, t).start())
            start([plane_a(d, t, slot_of(d, t), p) for p in range(3)])
            pair_a(dp, d, t, slot_of(d, t), 3).start()

        pl.when(valid(d, t))(arrived)
    for d, t in items:

        def arrived_f(d=d, t=t):
            for part in range(2):
                chain_f(d, t - 1, part).wait_recv()
                if t < 3:
                    pl.when(can[d])(lambda part=part: chain_f(d, t, part).start())
                plane_f(d, t, part).start()
                pair_f(d, t, slot_of(d, t), 0, part).start()

        pl.when(valid(d, t))(arrived_f)

    for p in range(3):
        plane_a(0, 0, 0, p).wait_recv()
        pair_a(peers[p], 0, 0, 0, p).start()
    for d, t in items:

        def spread(d=d, t=t):
            for part in range(2):
                plane_f(d, t, part).wait_recv()
                pair_f(d, t, slot_of(d, t), 1, part).start()
            for p in range(3):
                plane_a(d, t, slot_of(d, t), p).wait_recv()
                pair_a(peers[p], d, t, slot_of(d, t), p).start()

        pl.when(valid(d, t))(spread)

    for copy in own:
        copy.wait()
    for copy in own_pair:
        copy.wait()
    for p in range(3):
        plane_a(0, 0, 0, p).wait_send()
        pair_a(peers[p], 0, 0, 0, p).wait()
    for d in range(2):

        def sent(d=d):
            for copy in chain(d, 0):
                copy.wait_send()

        pl.when(can[d])(sent)
    for d, t in items:

        def done(d=d, t=t):
            slot = slot_of(d, t)
            if t < 3:

                def passed():
                    for copy in chain(d, t):
                        copy.wait_send()

                pl.when(can[d])(passed)
            for part in range(2):
                plane_f(d, t, part).wait_send()
                pair_f(d, t, slot, 0, part).wait()
                pair_f(d, t, slot, 1, part).wait()
            for p in range(3):
                plane_a(d, t, slot, p).wait_send()
            for p in range(4):
                pair_a(peers[p] if p < 3 else dp, d, t, slot, p).wait()

        pl.when(valid(d, t))(done)


def weights_of(f_shard, a_pair, cid):
    hbm = pl.BlockSpec(memory_space=pltpu.HBM)
    dma = pltpu.SemaphoreType.DMA
    kinds, _, lines, width = f_shard.shape
    blocks, rows, half = a_pair.shape
    return pl.pallas_call(
        gather_kernel,
        out_shape=(
            jax.ShapeDtypeStruct((kinds, 8, 2, lines, width), jnp.bfloat16),
            jax.ShapeDtypeStruct((blocks, 16, rows, half * 2), jnp.bfloat16),
        ),
        in_specs=[hbm, hbm],
        out_specs=(hbm, hbm),
        scratch_shapes=[
            dma((2,)),
            dma((2, 3, 2)), dma((2, 3, 2)),
            dma((2, 3, 2)), dma((2, 3, 2)),
            dma((7, 2, 2)), dma((7, 2, 2)),
            dma((2, 3)), dma((2, 3)),
            dma((7, 3)), dma((7, 3)),
            dma((7, 4)), dma((7, 4)),
        ],
        compiler_params=pltpu.CompilerParams(collective_id=cid, has_side_effects=True),
        name="gather_weights",
    )(f_shard, a_pair)


def attn_weight_kernel(count, *refs):
    *inputs, out = refs
    width = inputs[1].shape[1]
    spans = ((0, width), (width, 3 * width), (3 * width, 4 * width))
    for index, (first, last) in enumerate(spans):
        total = 0.0
        for n in range(count):
            total += dot_cols(inputs[6 * n + 2 * index][...], inputs[6 * n + 2 * index + 1][...])
        out[:, first:last] = total.astype(out.dtype)


def attn_weight_grad(uses, kind):
    return pl.pallas_call(
        functools.partial(attn_weight_kernel, len(uses)),
        out_shape=jax.ShapeDtypeStruct((uses[0][0].shape[1], 4 * uses[0][1].shape[1]), kind),
        compiler_params=pltpu.CompilerParams(vmem_limit_bytes=48 << 20),
        name="attn_weight_grad",
    )(*[value for use in uses for value in use])


def hidden_weight_kernel(small, left, left_small, right, right_small, out):
    total = dot_cols(left[...], right[...])
    if small:
        extra = dot_cols(left_small[...], right_small[...])
        total += jnp.where(pl.program_id(0) < small, extra, 0.0)
    out[...] = total.astype(out.dtype)


def hidden_weight_grad(parts, kind):
    (left, right), second = parts[0], parts[-1]
    tokens, units = left.shape
    block = math.gcd(second[0].shape[1], 512)
    small = second[0].shape[1] // block if len(parts) > 1 else 0
    whole = lambda value: pl.BlockSpec(value.shape, lambda i: (0, 0))
    last = second[0].shape[1] // block - 1
    return pl.pallas_call(
        functools.partial(hidden_weight_kernel, small),
        out_shape=jax.ShapeDtypeStruct((units, right.shape[1]), kind),
        grid=(units // block,),
        in_specs=[
            pl.BlockSpec((tokens, block), lambda i: (0, i)),
            pl.BlockSpec((tokens, block), lambda i: (0, jnp.minimum(i, last))),
            whole(right),
            whole(second[1]),
        ],
        out_specs=pl.BlockSpec((block, right.shape[1]), lambda i: (i, 0)),
        compiler_params=pltpu.CompilerParams(vmem_limit_bytes=48 << 20),
        name="hidden_weight_grad",
    )(left, second[0], right, second[1])


def reduce_kernel(*refs):
    hidden, attn, (hidden_out, attn_out) = refs[:4], refs[4:7], refs[7:9]
    own_f, own_a, sib_f, sib_a, plane_f, plane_a, far_f, far_a = refs[9:17]
    load_sem, pair_send, pair_recv, plane_send, plane_recv, far_send, far_recv = refs[17:]
    f32 = jnp.float32
    dp, wide = lax.axis_index("dp"), lax.axis_index("wide")
    level, core = wide // 2, wide % 2
    sibling = (dp, level * 2 + 1 - core)
    row, col = dp // 2, dp % 2
    peers = (row * 2 + 1 - col, (1 - row) * 2 + col, (1 - row) * 2 + 1 - col)
    far = [lax.rem(level + 1 + j, 4) for j in range(4)]

    barrier = pltpu.get_barrier_semaphore()
    partners = [sibling] + [(p, wide) for p in peers] + [(dp, far[j] * 2 + core) for j in range(3)]
    for device in partners:
        pl.semaphore_signal(barrier, inc=1, device_id=device, device_id_type=MESH)
    pl.semaphore_wait(barrier, len(partners))

    def remote(src, dst, send, recv, device):
        copy = pltpu.make_async_remote_copy(
            src_ref=src, dst_ref=dst, send_sem=send, recv_sem=recv, device_id=device, device_id_type=MESH
        )
        copy.start()
        return copy

    half = attn[0].shape[3] // 2

    def columns(side):
        return pl.ds(pl.multiple_of(side * half, 128), half)

    pair, loads = [], []
    for j in range(4):
        mine, theirs = far[j] * 2 + core, far[j] * 2 + 1 - core
        for k in range(4):
            pair.append(
                remote(hidden[k].at[theirs], sib_f.at[j, k], pair_send.at[j, k], pair_recv.at[j, k], sibling)
            )
            load = pltpu.make_async_copy(hidden[k].at[mine], own_f.at[j, k], load_sem.at[j, k])
            load.start()
            loads.append(load)
        for i in range(3):
            pair.append(
                remote(
                    attn[i].at[:, far[j], :, columns(1 - core)], sib_a.at[j, i], pair_send.at[j, 4 + i],
                    pair_recv.at[j, 4 + i], sibling,
                )
            )
            load = pltpu.make_async_copy(
                attn[i].at[:, far[j], :, columns(core)], own_a.at[j, i], load_sem.at[j, 4 + i]
            )
            load.start()
            loads.append(load)

    plane = []
    for j in range(4):
        for index in range(7):
            loads[7 * j + index].wait()
            pair[7 * j + index].wait_recv()

        def add_f(k, carry):
            for q in range(4):
                own_f[j, k, q] = (own_f[j, k, q].astype(f32) + sib_f[j, k, q].astype(f32)).astype(jnp.bfloat16)
            return carry

        lax.fori_loop(0, 4, add_f, 0)

        def add_a(q, carry):
            for i in range(3):
                own_a[j, i, q] = (own_a[j, i, q].astype(f32) + sib_a[j, i, q].astype(f32)).astype(jnp.bfloat16)
            return carry

        lax.fori_loop(0, 4, add_a, 0)
        sent = []
        for p, peer in enumerate(peers):
            sent.append(
                (
                    remote(own_f.at[j, :, peer], plane_f.at[j, p], plane_send.at[j, p, 0], plane_recv.at[j, p, 0], (peer, wide)),
                    remote(own_a.at[j, :, peer], plane_a.at[j, p], plane_send.at[j, p, 1], plane_recv.at[j, p, 1], (peer, wide)),
                )
            )
        plane.append(sent)

    flown = []
    for j in range(4):
        for sent in plane[j]:
            for copy in sent:
                copy.wait_recv()

        def total_f(k):
            total = own_f[j, k, dp].astype(f32)
            for p in range(3):
                total += plane_f[j, p, k].astype(f32)
            return total

        def total_a():
            total = own_a[j, :, dp].astype(f32)
            for p in range(3):
                total += plane_a[j, p].astype(f32)
            return total

        if j < 3:

            def keep(k, carry):
                plane_f[j, 0, k] = total_f(k).astype(jnp.bfloat16)
                return carry

            lax.fori_loop(0, 4, keep, 0)
            plane_a[j, 0] = total_a().astype(jnp.bfloat16)
            device = (dp, far[j] * 2 + core)
            flown.append(
                (
                    remote(plane_f.at[j, 0], far_f.at[j], far_send.at[j, 0], far_recv.at[j, 0], device),
                    remote(plane_a.at[j, 0], far_a.at[j], far_send.at[j, 1], far_recv.at[j, 1], device),
                )
            )
        else:

            def last(k, carry):
                hidden_out[k] = total_f(k)
                return carry

            lax.fori_loop(0, 4, last, 0)
            attn_out[...] = total_a()
    for j in range(3):
        for copy in flown[j]:
            copy.wait_recv()

        def finish(k, carry):
            hidden_out[k] += far_f[j, k].astype(f32)
            return carry

        lax.fori_loop(0, 4, finish, 0)
        attn_out[...] += far_a[j].astype(f32)
    for copy in pair:
        copy.wait_send()
    for sent in plane:
        for both in sent:
            for copy in both:
                copy.wait_send()
    for both in flown:
        for copy in both:
            copy.wait_send()


def reduced(hidden, attn, cid):
    _, _, rows, width = hidden[0].shape
    _, _, lines, columns = attn[0].shape
    block = (3, lines, columns // 2)
    bf = jnp.bfloat16
    hbm = pl.BlockSpec(memory_space=pltpu.HBM)
    vmem = pl.BlockSpec(memory_space=pltpu.VMEM)
    dma = pltpu.SemaphoreType.DMA
    return pl.pallas_call(
        reduce_kernel,
        out_shape=(
            jax.ShapeDtypeStruct((4, rows, width), jnp.float32),
            jax.ShapeDtypeStruct(block, jnp.float32),
        ),
        in_specs=[hbm] * 7,
        out_specs=(vmem, vmem),
        scratch_shapes=[
            pltpu.VMEM((4, 4, 4, rows, width), bf),
            pltpu.VMEM((4, 3, 4) + block[1:], bf),
            pltpu.VMEM((4, 4, 4, rows, width), bf),
            pltpu.VMEM((4, 3, 4) + block[1:], bf),
            pltpu.VMEM((4, 3, 4, rows, width), bf),
            pltpu.VMEM((4, 3) + block, bf),
            pltpu.VMEM((3, 4, rows, width), bf),
            pltpu.VMEM((3,) + block, bf),
            dma((4, 7)), dma((4, 7)), dma((4, 7)), dma((4, 3, 2)), dma((4, 3, 2)), dma((3, 2)), dma((3, 2)),
        ],
        compiler_params=pltpu.CompilerParams(
            collective_id=cid, has_side_effects=True, vmem_limit_bytes=56 << 20
        ),
        name="reduce_grads",
    )(*hidden, *attn)


def total_kernel(own, out, pair, plane, far, pair_send, pair_recv, plane_send, plane_recv, far_send, far_recv):
    dp, wide = lax.axis_index("dp"), lax.axis_index("wide")
    level, core = wide // 2, wide % 2
    row, col = dp // 2, dp % 2
    sibling = (dp, level * 2 + 1 - core)
    beside = (row * 2 + 1 - col, (1 - row) * 2 + col, (1 - row) * 2 + 1 - col)
    above = [lax.rem(level + 1 + j, 4) for j in range(3)]
    barrier = pltpu.get_barrier_semaphore()
    partners = [sibling] + [(p, wide) for p in beside] + [(dp, a * 2 + core) for a in above]
    for device in partners:
        pl.semaphore_signal(barrier, inc=1, device_id=device, device_id_type=MESH)
    pl.semaphore_wait(barrier, len(partners))

    def exchange(buffer, mine, value, others, devices, send, recv):
        buffer[mine] = value
        copies = [
            pltpu.make_async_remote_copy(
                src_ref=buffer.at[mine], dst_ref=buffer.at[mine], send_sem=send.at[n], recv_sem=recv.at[mine],
                device_id=device, device_id_type=MESH,
            )
            for n, device in enumerate(devices)
        ]
        for copy in copies:
            copy.start()
        for other, device in zip(others, devices):
            pltpu.make_async_remote_copy(
                src_ref=buffer.at[mine], dst_ref=buffer.at[other], send_sem=send.at[0], recv_sem=recv.at[other],
                device_id=device, device_id_type=MESH,
            ).wait_recv()
        total = buffer[0]
        for n in range(1, buffer.shape[0]):
            total += buffer[n]
        for copy in copies:
            copy.wait_send()
        return total

    total = exchange(pair, core, own[...], [1 - core], [sibling], pair_send, pair_recv)
    total = exchange(plane, dp, total, beside, [(p, wide) for p in beside], plane_send, plane_recv)
    out[...] = exchange(far, level, total, above, [(dp, a * 2 + core) for a in above], far_send, far_recv)


def total_of(own, cid):
    dma = pltpu.SemaphoreType.DMA
    vmem = lambda n: pltpu.VMEM((n,) + own.shape, own.dtype)
    return pl.pallas_call(
        total_kernel,
        out_shape=jax.ShapeDtypeStruct(own.shape, own.dtype),
        in_specs=[pl.BlockSpec(memory_space=pltpu.VMEM)],
        out_specs=pl.BlockSpec(memory_space=pltpu.VMEM),
        scratch_shapes=[
            vmem(2), vmem(4), vmem(4), dma((1,)), dma((2,)), dma((3,)), dma((4,)), dma((3,)), dma((4,)),
        ],
        compiler_params=pltpu.CompilerParams(collective_id=cid, has_side_effects=True),
        name="total_small",
    )(own)


def adamw(weight, first_m, second_m, grad_item, step_rate):
    first_new = beta_first * first_m + (1.0 - beta_first) * grad_item
    second_new = beta_second * second_m + (1.0 - beta_second) * grad_item * grad_item
    weight_new = weight - step_rate * (
        first_new / (jnp.sqrt(second_new) + adam_eps) + decay_weight * weight
    )
    return (weight_new, first_new, second_new)


def rows_of(source, row_start, number):
    return lax.dynamic_slice_in_dim(source, row_start, number, 0).reshape(-1)


def local(
    source_ids,
    token_ids,
    targets,
    pad_mask,
    pass_widths,
    attn_master,
    attn_m,
    attn_v,
    norm_params,
    norm_m,
    norm_v,
    up_master,
    up_m,
    up_v,
    down_master,
    down_m,
    down_v,
    embed_master,
    embed_m,
    embed_v,
    ema_old,
):
    wide_count = lax.axis_size("wide")
    wide_at = lax.axis_index("wide")
    dp_count = lax.axis_size("dp")
    dp_at = lax.axis_index("dp")
    model_width = norm_params.shape[1]
    length = token_ids.shape[1]
    seq_dev = token_ids.shape[0] // (wide_count * dp_count)
    tokens = seq_dev * length
    vocab_shard = embed_master.shape[0]
    planes = (dp_count, wide_count) == (4, 8)
    link_type = jnp.bfloat16 if planes else jnp.float32
    core = wide_at % 2
    swap = [(place, place ^ 1) for place in range(wide_count)]
    hidden_shards = jnp.stack(
        [up_master[0].T, down_master[0], up_master[1].T, down_master[1]]
    ).astype(jnp.bfloat16)
    attn_low = attn_master.astype(jnp.bfloat16)
    if planes:
        half = attn_low.shape[2] // 2
        other_low = lax.ppermute(attn_low, "wide", swap)
        pair_rows = jnp.concatenate(
            [jnp.where(core > 0, other_low, attn_low), jnp.where(core > 0, attn_low, other_low)],
            axis=1,
        )
        hidden_full, attn_full = weights_of(
            hidden_shards.reshape(4, 2, -1, model_width),
            lax.dynamic_slice_in_dim(pair_rows, core * half, half, 2),
            2,
        )
        hidden_full = hidden_full.reshape(4, -1, model_width)
        attn_full = attn_full.reshape(3, model_width, -1)
    else:
        attn_full = lax.all_gather(attn_low, ("dp", "wide"), axis=1, tiled=True)
        hidden_full = lax.all_gather(hidden_shards, "wide", axis=1, tiled=True)
    up_full, down_full = hidden_full[0::2], hidden_full[1::2]
    table_local = embed_master.astype(jnp.bfloat16)
    group_start = dp_at * wide_count * seq_dev
    own_start = group_start + wide_at * seq_dev
    count_all = jnp.sum(pad_mask).astype(jnp.float32)
    group_src = rows_of(source_ids, group_start, wide_count * seq_dev).reshape(wide_count, tokens)
    group_tgt = rows_of(token_ids, group_start, wide_count * seq_dev).reshape(wide_count, tokens)
    group_ids = jnp.concatenate([group_src, group_tgt], axis=1).reshape(-1)
    own_mask = rows_of(pad_mask, own_start, seq_dev).reshape(seq_dev, length) > 0
    free_mask = own_mask[:, None, None, :]
    causal = jnp.arange(length)[:, None] >= jnp.arange(length)[None, :]
    causal_mask = free_mask & causal[None, None]
    offset = wide_at * vocab_shard
    picked = group_ids - offset
    inside = (picked >= 0) & (picked < vocab_shard)
    found_rows = jnp.take(table_local, jnp.clip(picked, 0, vocab_shard - 1), axis=0).astype(
        jnp.float32
    )
    embedded = lax.psum_scatter(
        jnp.where(inside[:, None], found_rows, 0.0).astype(jnp.bfloat16),
        "wide",
        scatter_dimension=0,
        tiled=True,
    ).astype(jnp.float32)
    position = jnp.tile(sinusoid(length, model_width), (seq_dev, 1))
    src_in = math.sqrt(model_width) * embedded[:tokens] + position
    tgt_in = math.sqrt(model_width) * embedded[tokens:] + position

    def norm_at(values, index):
        return layer_norm(values, norm_params[index], norm_params[norm_count + index])

    src_val, source_norm_statistics = norm_at(src_in, 0)
    src_low = src_val.astype(jnp.bfloat16)
    src_att, src_kept = attn_forward(src_low, src_low, attn_full[0], free_mask, seq_dev)
    src_hidden = src_in + src_att
    sff_val, sff_stats = norm_at(src_hidden, 1)
    sff_low = sff_val.astype(jnp.bfloat16)
    src_inner = dot_rows(sff_low, up_full[0])
    tgt_val, tgt_stats = norm_at(tgt_in, 3)
    tgt_low = tgt_val.astype(jnp.bfloat16)
    tgt_att, tgt_kept = attn_forward(tgt_low, tgt_low, attn_full[1], causal_mask, seq_dev)
    tgt_hidden = tgt_in + tgt_att
    cross_val, cross_stats = norm_at(tgt_hidden, 4)
    cross_low = cross_val.astype(jnp.bfloat16)
    passes = []
    final_list = []
    pass_units = (up_full.shape[1], up_full.shape[1] // 2)
    for pass_index in range(2):
        held = pass_units[pass_index]
        enc_out, enc_active, enc_act = ffn_pass(
            src_hidden, src_inner, down_full[0, :held], pass_widths[pass_index]
        )
        mem_val, mem_stats = norm_at(enc_out, 2)
        mem_low = mem_val.astype(jnp.bfloat16)
        x_att, x_kept = attn_forward(cross_low, mem_low, attn_full[2], free_mask, seq_dev)
        crossed = tgt_hidden + x_att
        dff_val, dff_stats = norm_at(crossed, 5)
        dff_low = dff_val.astype(jnp.bfloat16)
        dec_inner = dot_rows(dff_low, up_full[1, :held])
        dec_out, dec_active, dec_act = ffn_pass(
            crossed, dec_inner, down_full[1, :held], pass_widths[pass_index]
        )
        fin_val, fin_stats = norm_at(dec_out, 6)
        passes.append(
            (
                enc_active,
                enc_act,
                mem_stats,
                x_kept,
                dff_stats,
                dff_low,
                dec_active,
                dec_act,
                fin_stats,
            )
        )
        final_list.append(fin_val.astype(jnp.bfloat16))
    final_pair = (final_list[0], final_list[1])
    gathered = (
        lax.all_gather(final_pair[0], "wide", axis=0, tiled=True),
        lax.all_gather(final_pair[1], "wide", axis=0, tiled=True),
    )
    head_in = jnp.concatenate(gathered, axis=0)
    row_targets = jnp.tile(rows_of(targets, group_start, wide_count * seq_dev), 2)
    row_masks = jnp.tile(
        rows_of(pad_mask, group_start, wide_count * seq_dev).astype(jnp.float32), 2
    )
    chunk = math.gcd(head_in.shape[0], 4096)
    chunks = [slice(at, at + chunk) for at in range(0, head_in.shape[0], chunk)]
    exps, stats = zip(
        *[head_stats(head_in[at], row_targets[at], table_local, offset) for at in chunks]
    )
    stats = jnp.concatenate(stats, axis=2)
    tile_peaks = stats[:, 0]
    own_peak = jnp.max(tile_peaks, axis=0)
    own_total = jnp.sum(stats[:, 1] * jnp.exp(tile_peaks - own_peak), axis=0)
    row_peak, row_total, target_logit, logit_sum = merged(
        (own_peak, own_total, jnp.sum(stats[:, 2], axis=0), jnp.sum(stats[:, 3], axis=0)), "wide"
    )
    row_weights = row_masks / count_all
    log_total = row_peak + jnp.log(row_total)
    row_error = log_total - (1.0 - smooth) * target_logit - smooth / V * logit_sum
    row_loss = (row_weights * row_error).reshape(2, -1)
    row_plain = (row_masks * row_error).reshape(2, -1)
    scale = (row_weights * jnp.exp(tile_peaks - log_total))[:, None, :]
    row_grads, table_grad = zip(
        *[
            head_grads(
                head_in[at], row_targets[at], row_weights[at], scale[:, :, at], part,
                table_local.T, offset,
            )
            for at, part in zip(chunks, exps)
        ]
    )
    row_grads, table_grad = jnp.concatenate(row_grads), sum(table_grad)
    half_rows = head_in.shape[0] // 2
    loss_own = jnp.sum(lax.dynamic_slice_in_dim(row_loss, wide_at * tokens, tokens, 1), axis=1)
    plain_own = lax.dynamic_slice_in_dim(row_plain, wide_at * tokens, tokens, 1)
    final_grads = (
        lax.psum_scatter(
            row_grads[:half_rows], "wide", scatter_dimension=0, tiled=True
        ).astype(jnp.float32),
        lax.psum_scatter(
            row_grads[half_rows:], "wide", scatter_dimension=0, tiled=True
        ).astype(jnp.float32),
    )
    row_losses = plain_own.reshape(2, seq_dev, length)
    gain_parts = [jnp.zeros((model_width,), jnp.float32) for index in range(norm_count)]
    shift_parts = [jnp.zeros((model_width,), jnp.float32) for index in range(norm_count)]

    def backward_layer_norm(upstream, stats, index):
        back, gain_part, shift_part = norm_back(upstream, stats, norm_params[index])
        gain_parts[index] = gain_parts[index] + gain_part
        shift_parts[index] = shift_parts[index] + shift_part
        return back

    src_inner_grad = jnp.zeros(src_inner.shape, jnp.float32)
    source_hidden_gradient = jnp.zeros((tokens, model_width), jnp.float32)
    tgt_hidden_grad = jnp.zeros((tokens, model_width), jnp.float32)
    cross_grad = jnp.zeros((tokens, model_width), jnp.float32)
    cross_weight = []
    up_grads = [[], []]
    down_grads = [[], []]
    for pass_index in range(2):
        (
            enc_active,
            enc_act,
            mem_stats,
            x_kept,
            dff_stats,
            dff_low,
            dec_active,
            dec_act,
            fin_stats,
        ) = passes[pass_index]
        out_grad = backward_layer_norm(final_grads[pass_index], fin_stats, 6)
        out_low = out_grad.astype(jnp.bfloat16)
        held = pass_units[pass_index]
        down_grads[1].append((dec_act, out_low))
        dec_low = jnp.where(
            dec_active, dot_rows(out_low, down_full[1, :held]), 0.0
        ).astype(jnp.bfloat16)
        up_grads[1].append((dec_low, dff_low))
        crossed_grad = out_grad + backward_layer_norm(
            jnp.dot(dec_low, up_full[1, :held], preferred_element_type=jnp.float32), dff_stats, 5
        )
        query_in, memory_in, block_grad = attention_backward_pass(
            x_kept, crossed_grad.astype(jnp.bfloat16), attn_full[2]
        )
        cross_weight.append(block_grad)
        tgt_hidden_grad = tgt_hidden_grad + crossed_grad
        cross_grad = cross_grad + query_in
        enc_grad = backward_layer_norm(memory_in, mem_stats, 2)
        enc_low = enc_grad.astype(jnp.bfloat16)
        down_grads[0].append((enc_act, enc_low))
        src_inner_grad = src_inner_grad + jnp.pad(
            jnp.where(enc_active, dot_rows(enc_low, down_full[0, :held]), 0.0),
            ((0, 0), (0, src_inner.shape[1] - held)),
        )
        source_hidden_gradient = source_hidden_gradient + enc_grad
    tgt_hidden_grad = tgt_hidden_grad + backward_layer_norm(cross_grad, cross_stats, 4)
    src_inner_low = src_inner_grad.astype(jnp.bfloat16)
    up_grads[0].append((src_inner_low, sff_low))
    source_hidden_gradient = source_hidden_gradient + backward_layer_norm(
        jnp.dot(src_inner_low, up_full[0], preferred_element_type=jnp.float32), sff_stats, 1
    )
    tq_in, tkv_in, tgt_weight = attention_backward_pass(
        tgt_kept, tgt_hidden_grad.astype(jnp.bfloat16), attn_full[1]
    )
    tgt_in_grad = tgt_hidden_grad + backward_layer_norm(tq_in + tkv_in, tgt_stats, 3)
    source_query_input, source_key_value_input, source_norm_weight = attention_backward_pass(
        src_kept, source_hidden_gradient.astype(jnp.bfloat16), attn_full[0]
    )
    source_input_gradient = source_hidden_gradient + backward_layer_norm(
        source_query_input + source_key_value_input, source_norm_statistics, 0
    )
    hidden_grads = [
        hidden_weight_grad(parts, link_type)
        for parts in (down_grads[1], up_grads[1], down_grads[0], up_grads[0])
    ]
    attn_grads = [
        attn_weight_grad(uses, link_type)
        for uses in ([source_norm_weight], [tgt_weight], cross_weight)
    ]
    norm_grad = jnp.stack(gain_parts + shift_parts)
    embed_low = (
        math.sqrt(model_width) * jnp.concatenate([source_input_gradient, tgt_in_grad], axis=0)
    ).astype(jnp.bfloat16)
    spread_rows = lax.all_gather(embed_low, "wide", axis=0, tiled=True)
    local_ids = group_ids - offset
    inside_rows = (local_ids >= 0) & (local_ids < vocab_shard)
    embed_part = table_grad.at[jnp.clip(local_ids, 0, vocab_shard - 1)].add(
        jnp.where(inside_rows[:, None], spread_rows.astype(jnp.float32), 0.0)
    )
    if planes:
        hidden_part, attn_part = reduced(
            [part.reshape(wide_count, dp_count, -1, model_width) for part in hidden_grads],
            [part.reshape(4, 4, -1, part.shape[1]) for part in attn_grads],
            1,
        )
        lines = attn_master.shape[1]
        mine = lax.dynamic_slice_in_dim(attn_part, core * lines, lines, 1)
        other = lax.ppermute(
            lax.dynamic_slice_in_dim(attn_part, (1 - core) * lines, lines, 1), "wide", swap
        )
        attn_shard = jnp.concatenate(
            [jnp.where(core > 0, other, mine), jnp.where(core > 0, mine, other)], axis=2
        )
        hidden_sum = jnp.moveaxis(
            lax.all_gather(hidden_part.astype(link_type), "dp"), 0, 1
        ).reshape(4, -1, model_width).astype(jnp.float32)
        square_part = jnp.sum(hidden_part * hidden_part)
    else:
        hidden_sum = lax.psum(
            jnp.stack(
                [
                    lax.psum_scatter(part, "wide", scatter_dimension=0, tiled=True)
                    for part in hidden_grads
                ]
            ),
            "dp",
        )
        square_part = jnp.sum(hidden_sum * hidden_sum) / dp_count
        attn_shard = lax.psum_scatter(
            jnp.stack(attn_grads), ("dp", "wide"), scatter_dimension=1, tiled=True
        )
    embed_sum = lax.psum(embed_part.astype(jnp.bfloat16), "dp").astype(jnp.float32)
    down_sum = jnp.stack([hidden_sum[2], hidden_sum[0]])
    up_sum = jnp.stack([hidden_sum[3].T, hidden_sum[1].T])
    square_part += (
        jnp.sum(attn_shard * attn_shard) + jnp.sum(embed_sum * embed_sum) / dp_count
    )
    if planes:
        flat = jnp.concatenate([norm_grad.reshape(-1), loss_own, square_part.reshape(1)])
        flat = total_of(jnp.pad(flat, (0, -flat.size % 1024)).reshape(-1, 128), 3).reshape(-1)
        norm_sum = flat[: norm_grad.size].reshape(norm_grad.shape)
        losses, square_all = flat[norm_grad.size :][:2], flat[norm_grad.size + 2]
    else:
        square_all, norm_sum, losses = lax.psum(
            (square_part, norm_grad, loss_own), ("dp", "wide")
        )
    grad_norm = jnp.sqrt(square_all + jnp.sum(norm_sum * norm_sum))
    clip_scale = clip_limit / jnp.maximum(grad_norm, clip_limit)
    attn_new, attn_m_new, attn_v_new = adamw(
        attn_master, attn_m, attn_v, clip_scale * attn_shard, rate_matrix
    )
    norm_new, norm_m_new, norm_v_new = adamw(
        norm_params, norm_m, norm_v, clip_scale * norm_sum, rate_gains
    )
    up_new, up_m_new, up_v_new = adamw(up_master, up_m, up_v, clip_scale * up_sum, rate_matrix)
    down_new, down_m_new, down_v_new = adamw(
        down_master, down_m, down_v, clip_scale * down_sum, rate_matrix
    )
    embed_new, embed_m_new, embed_v_new = adamw(
        embed_master, embed_m, embed_v, clip_scale * embed_sum, rate_matrix
    )
    ema_cols = ema_old.shape[1]
    ema_new = ema_decay * ema_old + (1.0 - ema_decay) * lax.dynamic_slice_in_dim(
        embed_new, dp_at * ema_cols, ema_cols, 1
    )
    return (
        losses,
        row_losses,
        grad_norm.reshape(1),
        attn_new,
        attn_m_new,
        attn_v_new,
        norm_new,
        norm_m_new,
        norm_v_new,
        up_new,
        up_m_new,
        up_v_new,
        down_new,
        down_m_new,
        down_v_new,
        embed_new,
        embed_m_new,
        embed_v_new,
        ema_new,
        attn_new.astype(jnp.bfloat16),
        up_new.astype(jnp.bfloat16),
        down_new.astype(jnp.bfloat16),
        embed_new.astype(jnp.bfloat16),
    )


def solution(mesh):
    in_specs = (
        P(),
        P(),
        P(),
        P(),
        P(),
        P(None, ("dp", "wide"), None),
        P(None, ("dp", "wide"), None),
        P(None, ("dp", "wide"), None),
        P(),
        P(),
        P(),
        P(None, None, "wide"),
        P(None, None, "wide"),
        P(None, None, "wide"),
        P(None, "wide", None),
        P(None, "wide", None),
        P(None, "wide", None),
        P("wide", None),
        P("wide", None),
        P("wide", None),
        P("wide", "dp"),
    )
    out_specs = (
        P(),
        P(None, ("dp", "wide"), None),
        P(),
        P(None, ("dp", "wide"), None),
        P(None, ("dp", "wide"), None),
        P(None, ("dp", "wide"), None),
        P(),
        P(),
        P(),
        P(None, None, "wide"),
        P(None, None, "wide"),
        P(None, None, "wide"),
        P(None, "wide", None),
        P(None, "wide", None),
        P(None, "wide", None),
        P("wide", None),
        P("wide", None),
        P("wide", None),
        P("wide", "dp"),
        P(None, ("dp", "wide"), None),
        P(None, None, "wide"),
        P(None, "wide", None),
        P("wide", None),
    )
    return jax.shard_map(local, mesh=mesh, in_specs=in_specs, out_specs=out_specs, check_vma=False)
```
